128 devices in a mesh: gx: 8 (over z, core), gy: 16 (over y, x).
Axes of the slice: x: 4, y: 4, z: 4, core: 2. Of those that a mesh axis runs over, the one named last changes fastest.
Arguments:
- points: bfloat16 [1, 131072, 256], P(None, ('gx', 'gy')), may hold values from -16 to 16
- send_rows: int32 [1, 128, 768], P(None, ('gx', 'gy')), may hold values from 0 to 1023, as said below
- recv_slot: int32 [1, 131072], P(None, ('gx', 'gy')), may hold values from 0 to 1791, as said below
- norm1_gain: float32 [256], replicated, may hold values from 0.1 to 1.9
- qkv_weight: bfloat16 [256, 768], replicated, may hold values from -0.375 to 0.375
- proj_weight: bfloat16 [256, 256], replicated, may hold values from -0.375 to 0.375
- norm2_gain: float32 [256], replicated, may hold values from 0.1 to 1.9
- fc1_weight: bfloat16 [256, 1024], replicated, may hold values from -0.375 to 0.375
- fc2_weight: bfloat16 [1024, 256], replicated, may hold values from -0.1875 to 0.1875
- cotangent: bfloat16 [1, 131072, 256], P(None, ('gx', 'gy')), may hold values from -6 to 6
Outputs:
- block_out: bfloat16 [1, 131072, 256], P(None, ('gx', 'gy'))
- grad_points: bfloat16 [1, 131072, 256], P(None, ('gx', 'gy'))
The draws below stay inside these ranges and needn't reach their ends.
Inputs may be any that keep to these rules, and one draw needn't show every extreme that they name: `send_rows`: for every event and source device a, the first L(a) of the slots toward a - 1 and the first R(a) of the slots toward a + 1 (devices mod 128) are used; the rows they name are distinct and, with the rows that recv_slot of device a lists as its own, cover all 1024 rows of a. Unused slots name arbitrary rows. L(a) and R(a) are at most 384, and in every event some device sends exactly 384 points to its next device. `recv_slot`: for every event and destination device d, the 1024 entries of d's block are distinct: a value s < 1024 names d's own z-order row s, 1024 + c the c-th slot of device d - 1 toward d, 1408 + c the c-th slot of device d + 1 toward d (mod 128); exactly the used slots appear, so that the Hilbert order is a permutation of the z-order in which every point moves at most one device along the curve.
All inputs are finite; a program needn't handle non-finite values.
Results may differ from the reference program's by a relative error of at most 0.0054.
Values may be sent and summed in bfloat16 or wider, within the bound.
No kernel may reach another device: no remote copies, remote signals or barrier semaphores. Data moves between devices by JAX's collectives and lax.ppermute only.
A program may use at most 128 MiB of HBM per device.

```python
import math
import jax
import jax.numpy as jnp
from jax import lax

C = 256
H = 16
FF = 1024
K = 1024
P_DEV = 1024
EVENTS = 1
HD = 256
SHIFT = 512
NPTS = 131072
CAP = 384
DEVICES = 128


def routing_plan(key, event_index):
    quarter = P_DEV // 4
    eighth = P_DEV // 8
    event_key = jax.random.fold_in(jax.random.fold_in(key, 4242), event_index)
    subkeys = jax.random.split(event_key, 4)
    device_ids = jnp.arange(DEVICES, dtype=jnp.int32)
    twist = jax.random.randint(subkeys[0], (DEVICES,), 0, eighth + 1).astype(jnp.int32)
    pinned = jax.random.randint(subkeys[1], (), 0, DEVICES).astype(jnp.int32)
    twist = jnp.where(device_ids == pinned, eighth, twist).astype(jnp.int32)
    before = twist[(device_ids - 1 + DEVICES) % DEVICES]
    left_count = quarter + before
    right_count = quarter + twist
    row_orders = jax.vmap(lambda source_id: jax.random.permutation(jax.random.fold_in(subkeys[2], source_id), P_DEV))(device_ids).astype(jnp.int32)
    slot_ids = jnp.arange(CAP, dtype=jnp.int32)
    left_rows = row_orders[:, :CAP]
    right_pos = (P_DEV - right_count[:, None] + slot_ids[None, :]) % P_DEV
    right_rows = jnp.take_along_axis(row_orders, right_pos, axis=1)
    send_table = jnp.concatenate([left_rows, right_rows], axis=1)
    rank_ids = jnp.arange(P_DEV, dtype=jnp.int32)

    def place_rows(dest_id):
        own_left = left_count[dest_id]
        keep = P_DEV - own_left - right_count[dest_id]
        from_prev = right_count[(dest_id - 1 + DEVICES) % DEVICES]
        own_rows = row_orders[dest_id][jnp.clip(own_left + rank_ids, 0, P_DEV - 1)]
        entries = jnp.where(rank_ids < keep, own_rows, jnp.where(rank_ids < keep + from_prev, P_DEV + rank_ids - keep, P_DEV + CAP + rank_ids - keep - from_prev))
        shuffle = jax.random.permutation(jax.random.fold_in(subkeys[3], dest_id), P_DEV)
        return entries[shuffle]
    slot_table = jax.vmap(place_rows)(device_ids).reshape(DEVICES * P_DEV)
    return (send_table.astype(jnp.int32), slot_table.astype(jnp.int32))


def draw_send_rows(key, part):
    return jax.vmap(lambda event_index: routing_plan(key, event_index)[0])(jnp.arange(EVENTS, dtype=jnp.int32))


def draw_recv_slot(key, part):
    return jax.vmap(lambda event_index: routing_plan(key, event_index)[1])(jnp.arange(EVENTS, dtype=jnp.int32))


def draw_points(key, part):
    subkeys = jax.random.split(jax.random.fold_in(key, 99), 2)
    row_scale = jnp.exp(jax.random.uniform(subkeys[1], (EVENTS, NPTS, 1), minval=math.log(0.5), maxval=math.log(4.0)))
    base_values = jnp.clip(jax.random.normal(subkeys[0], (EVENTS, NPTS, C)), -4.0, 4.0)
    return (base_values * row_scale).astype(jnp.float32).astype(jnp.bfloat16)


def level_of(stream_key, extent, cuts, smallest, top_value):
    def one(dim, blocks):
        heights = jax.random.uniform(jax.random.fold_in(jax.random.fold_in(stream_key, 6), dim), (blocks,), jnp.float32, smallest / len(cuts), top_value / len(cuts))
        return jnp.repeat(jnp.exp(heights), extent[dim] // blocks).reshape((-1,) + (1,) * (len(extent) - dim - 1))

    level = one(*cuts[0])
    for cut in cuts[1:]:
        level = level * one(*cut)
    return level


def normal_values(stream_key, shape, scale, bound, cuts=(), kind=jnp.bfloat16):
    factor_of = level_of(stream_key, shape, cuts, -0.22, 0.18) if cuts else 1.0
    drawn = jax.random.normal(stream_key, shape, jnp.float32) * scale * factor_of
    return jnp.minimum(jnp.maximum(drawn, -bound), bound).astype(kind)


def setup_inputs(seed: int = 0) -> dict:
    seeds = jax.random.split(jax.random.key(seed), 11)
    return {
        "points": draw_points(jax.random.fold_in(seeds[10], 71), 0),
        "send_rows": draw_send_rows(jax.random.fold_in(seeds[10], 71), 0),
        "recv_slot": draw_recv_slot(jax.random.fold_in(seeds[10], 71), 0),
        "norm1_gain": jnp.clip(1.0 + 0.18 * jax.random.normal(seeds[3], (C,), jnp.float32), 0.1, 1.9),
        "qkv_weight": normal_values(seeds[4], (C, 3 * HD), C ** -0.5, 0.375),
        "proj_weight": normal_values(seeds[5], (HD, C), HD ** -0.5, 0.375),
        "norm2_gain": jnp.clip(1.0 + 0.18 * jax.random.normal(seeds[6], (C,), jnp.float32), 0.1, 1.9),
        "fc1_weight": normal_values(seeds[7], (C, FF), C ** -0.5, 0.375),
        "fc2_weight": normal_values(seeds[8], (FF, C), FF ** -0.5, 0.1875),
        "cotangent": normal_values(seeds[9], (EVENTS, NPTS, C), 1.0, 6.0, ((1, 128),)),
    }


epsilon = 1e-05

def norm_rows(row_block, gain):
    row_mean = lax.optimization_barrier(jnp.mean(row_block, axis=-1, keepdims=True))
    centered = row_block - row_mean
    spread = lax.optimization_barrier(jnp.mean(centered * centered, axis=-1, keepdims=True))
    return centered * lax.rsqrt(spread + epsilon) * gain

def gelu_exact(values):
    return jax.nn.gelu(values, approximate=False)

def front(ordered, norm1_gain, qkv_weight):
    normed = norm_rows(ordered.astype(jnp.float32), norm1_gain).astype(jnp.bfloat16)
    return jnp.dot(normed, qkv_weight, preferred_element_type=jnp.float32).astype(jnp.bfloat16)

def rest_pass(ordered, attention, norm2_gain, proj_weight, fc1_weight, fc2_weight, cotangent):
    mixed_rows = ordered.astype(jnp.float32) + jnp.dot(attention, proj_weight, preferred_element_type=jnp.float32)
    normed_two, norm_back = jax.vjp(lambda row_block: norm_rows(row_block, norm2_gain), mixed_rows)
    hidden_pre = jnp.dot(normed_two.astype(jnp.bfloat16), fc1_weight, preferred_element_type=jnp.float32)
    activated, gelu_back = jax.vjp(gelu_exact, hidden_pre)
    activated_b = activated.astype(jnp.bfloat16)
    block_out = (mixed_rows + jnp.dot(activated_b, fc2_weight, preferred_element_type=jnp.float32)).astype(jnp.bfloat16)
    grad_act = jnp.dot(cotangent, fc2_weight.T, preferred_element_type=jnp.float32)
    grad_pre = gelu_back(grad_act)[0].astype(jnp.bfloat16)
    grad_normed = jnp.dot(grad_pre, fc1_weight.T, preferred_element_type=jnp.float32)
    grad_mixed = cotangent.astype(jnp.float32) + norm_back(grad_normed)[0]
    grad_attention = jnp.dot(grad_mixed.astype(jnp.bfloat16), proj_weight.T, preferred_element_type=jnp.float32).astype(jnp.bfloat16)
    return (block_out, grad_attention, grad_mixed)

def front_backward(ordered, grad_qkv, grad_mixed, norm1_gain, qkv_weight):
    unused, norm_back = jax.vjp(lambda row_block: norm_rows(row_block, norm1_gain), ordered.astype(jnp.float32))
    grad_normed = jnp.dot(grad_qkv.astype(jnp.bfloat16), qkv_weight.T, preferred_element_type=jnp.float32)
    return (grad_mixed + norm_back(grad_normed)[0]).astype(jnp.bfloat16)

def split_heads(matrix, head_count):
    return matrix.astype(jnp.float32).reshape(matrix.shape[0], head_count, matrix.shape[1] // head_count)

def attend(queries, key_rows, value_rows, head_count):
    row_count = queries.shape[0]
    head_size = queries.shape[1] // head_count
    score_scale = 1.0 / math.sqrt(head_size)
    query_heads = split_heads(queries, head_count)
    key_heads = split_heads(key_rows, head_count)
    value_heads = split_heads(value_rows, head_count)
    scores = jnp.einsum('qhd,khd->hqk', query_heads, key_heads) * score_scale
    weights = jnp.exp(scores)
    probs_b = (weights / lax.optimization_barrier(jnp.sum(weights, axis=-1, keepdims=True))).astype(jnp.bfloat16)
    result = jnp.einsum('hqk,khd->qhd', probs_b.astype(jnp.float32), value_heads)
    return result.reshape(row_count, -1).astype(jnp.bfloat16)

def attend_backward(queries, key_rows, value_rows, grad_out, head_count):
    row_count = queries.shape[0]
    window = key_rows.shape[0]
    head_size = queries.shape[1] // head_count
    score_scale = 1.0 / math.sqrt(head_size)
    query_heads = split_heads(queries, head_count)
    key_heads = split_heads(key_rows, head_count)
    value_heads = split_heads(value_rows, head_count)
    grad_heads = split_heads(grad_out, head_count)
    scores = jnp.einsum('qhd,khd->hqk', query_heads, key_heads) * score_scale
    weights = jnp.exp(scores)
    probs_full = weights / lax.optimization_barrier(jnp.sum(weights, axis=-1, keepdims=True))
    probs_b = probs_full.astype(jnp.bfloat16).astype(jnp.float32)
    grad_probs = jnp.einsum('qhd,khd->hqk', grad_heads, value_heads)
    grad_values = jnp.einsum('hqk,qhd->khd', probs_b, grad_heads)
    inner_sum = lax.optimization_barrier(jnp.sum(probs_full * grad_probs, axis=-1, keepdims=True))
    grad_scores = (probs_full * (grad_probs - inner_sum) * score_scale).astype(jnp.bfloat16).astype(jnp.float32)
    grad_queries = jnp.einsum('hqk,khd->qhd', grad_scores, key_heads)
    grad_keys = jnp.einsum('hqk,qhd->khd', grad_scores, query_heads)
    grad_window = jnp.concatenate([grad_keys.reshape(window, -1), grad_values.reshape(window, -1)], axis=1)
    return (grad_queries.reshape(row_count, -1), grad_window)

def by_blocks(matrix):
    return matrix.reshape((DEVICES, P_DEV) + matrix.shape[1:])

def unblock(matrix):
    return matrix.reshape((NPTS,) + matrix.shape[2:])

def reference(points, send_rows, recv_slot, norm1_gain, qkv_weight, proj_weight, norm2_gain, fc1_weight, fc2_weight, cotangent):
    outputs_list = []
    grads_list = []
    positions = jnp.arange(NPTS, dtype=jnp.int32)
    target = (positions // P_DEV).astype(jnp.int32)
    prev_dev = ((target - 1 + DEVICES) % DEVICES).astype(jnp.int32)
    next_dev = ((target + 1) % DEVICES).astype(jnp.int32)
    patch_count = NPTS // K
    for event_index in range(EVENTS):
        slot_ids = recv_slot[event_index].astype(jnp.int32)
        rows_table = send_rows[event_index]
        from_self = slot_ids < P_DEV
        from_prev = jnp.logical_and(slot_ids >= P_DEV, slot_ids < P_DEV + CAP)
        own_row = jnp.clip(slot_ids, 0, P_DEV - 1).astype(jnp.int32)
        prev_pos = jnp.clip(slot_ids - P_DEV, 0, CAP - 1).astype(jnp.int32)
        next_pos = jnp.clip(slot_ids - P_DEV - CAP, 0, CAP - 1).astype(jnp.int32)
        prev_row = rows_table[prev_dev, CAP + prev_pos]
        next_row = rows_table[next_dev, next_pos]
        curve_index = jnp.where(from_self, target * P_DEV + own_row, jnp.where(from_prev, prev_dev * P_DEV + prev_row, next_dev * P_DEV + next_row)).astype(jnp.int32)
        ordered = points[event_index][curve_index]
        qkv = unblock(lax.map(lambda row_block: front(row_block, norm1_gain, qkv_weight), by_blocks(ordered)))
        queries = qkv[:, :HD]
        key_values = qkv[:, HD:]
        rolled_q = jnp.roll(queries, SHIFT, axis=0).reshape(patch_count, K, HD)
        rolled_kv = jnp.roll(key_values, SHIFT, axis=0).reshape(patch_count, K, 2 * HD)
        attention = lax.map(lambda pair: attend(pair[0], pair[1][:, :HD], pair[1][:, HD:], H), (rolled_q, rolled_kv))
        attention = jnp.roll(attention.reshape(NPTS, HD), -SHIFT, axis=0)
        block_out, grad_attention, grad_mixed = lax.map(lambda trio: rest_pass(trio[0], trio[1], norm2_gain, proj_weight, fc1_weight, fc2_weight, trio[2]), (by_blocks(ordered), by_blocks(attention), by_blocks(cotangent[event_index])))
        block_out = unblock(block_out)
        grad_attention = unblock(grad_attention)
        grad_mixed = unblock(grad_mixed)
        rolled_g = jnp.roll(grad_attention, SHIFT, axis=0).reshape(patch_count, K, HD)
        grad_q, grad_kv = lax.map(lambda trio: attend_backward(trio[0], trio[1][:, :HD], trio[1][:, HD:], trio[2], H), (rolled_q, rolled_kv, rolled_g))
        grad_qkv = jnp.concatenate([grad_q.reshape(NPTS, HD), grad_kv.reshape(NPTS, 2 * HD)], axis=1)
        grad_qkv = jnp.roll(grad_qkv, -SHIFT, axis=0)
        grad_ordered = unblock(lax.map(lambda trio: front_backward(trio[0], trio[1], trio[2], norm1_gain, qkv_weight), (by_blocks(ordered), by_blocks(grad_qkv), by_blocks(grad_mixed))))
        grad_event = jnp.zeros((NPTS, C), jnp.bfloat16).at[curve_index].set(grad_ordered)
        outputs_list.append(block_out)
        grads_list.append(grad_event)
    return (jnp.stack(outputs_list), jnp.stack(grads_list))
```

```python
import functools
import math

import jax
import jax.numpy as jnp
from jax import lax
from jax.experimental import pallas as pl
from jax.experimental.pallas import tpu as pltpu
from jax.sharding import PartitionSpec as P

H = 16
D = 16
C = 256
N = 1024
HALF = 512
CAP = 384
FF = 1024
ROWS = 256
EPS = 1e-05
LOG2E = 1.4426950408889634
SCORE = LOG2E / 4.0
VSCALE = 2.0**-8

bf16 = jnp.bfloat16
f32 = jnp.float32


def dg(a, b, ca, cb):
    return lax.dot_general(a, b, (((ca,), (cb,)), ((), ())), preferred_element_type=f32)


def column(row, count):
    return jnp.transpose(jnp.broadcast_to(row, (128, count)))


def picks_from_column(col, start, width):
    lanes = lax.broadcasted_iota(jnp.int32, col.shape, 1)
    parts = [
        jnp.where(col == lanes + (start + 128 * b), 1.0, 0.0).astype(bf16)
        for b in range(width // 128)
    ]
    return jnp.concatenate(parts, axis=1)


def picks_from_row(row, start, height):
    ids = lax.broadcasted_iota(jnp.int32, (height, row.shape[1]), 0) + start
    return jnp.where(ids == row, 1.0, 0.0).astype(bf16)


def gather_kernel(points, sender, left, right):
    col = column(sender[...], 2 * CAP)
    rows = dg(picks_from_column(col, 0, N), points[...], 1, 0).astype(bf16)
    left[...] = rows[:CAP]
    right[...] = rows[CAP:]


def order_kernel(points, from_prev, from_next, slot, first, second):
    col = column(slot[...], N)
    rows = dg(picks_from_column(col, 0, N), points[...], 1, 0)
    rows += dg(picks_from_column(col, N, CAP), from_prev[...], 1, 0)
    rows += dg(picks_from_column(col, N + CAP, CAP), from_next[...], 1, 0)
    rows = rows.astype(bf16)
    first[...] = rows[:HALF]
    second[...] = rows[HALF:]


def back_kernel(first, second, slot, to_prev, to_next):
    row = slot[...]
    picks = picks_from_row(row, N, 2 * CAP)
    rows = dg(picks[:, :HALF], first[...], 1, 0) + dg(picks[:, HALF:], second[...], 1, 0)
    rows = rows.astype(bf16)
    to_prev[...] = rows[:CAP]
    to_next[...] = rows[CAP:]


def own_kernel(first, second, slot, out):
    picks = picks_from_row(slot[...], 0, N)
    rows = dg(picks[:, :HALF], first[...], 1, 0) + dg(picks[:, HALF:], second[...], 1, 0)
    out[...] = rows.astype(bf16)


def final_kernel(own, left, right, sender, out):
    picks = picks_from_row(sender[...], 0, N)
    rows = dg(picks[:, :CAP], left[...], 1, 0) + dg(picks[:, CAP:], right[...], 1, 0)
    out[...] = (own[...].astype(f32) + rows).astype(bf16)


def normalize(rows):
    mean = jnp.mean(rows, axis=-1, keepdims=True)
    centered = rows - mean
    spread = jnp.mean(centered * centered, axis=-1, keepdims=True)
    scale = lax.rsqrt(spread + EPS)
    return centered * scale, scale


def normalize_back(grad, unit, scale):
    return scale * (
        grad
        - jnp.mean(grad, axis=-1, keepdims=True)
        - unit * jnp.mean(grad * unit, axis=-1, keepdims=True)
    )


def main_kernel(
    ord_lo, ord_hi, cot_lo, cot_hi, gain1, wqkv, wproj, gain2, wfc1, wfc2,
    out_lo, out_hi, grad_lo, grad_hi,
    e_scr, x_scr, kn, vn, qt, kt, vt, ot, inv_scr, amp_scr, gt, mix_grad, dt,
):
    x_scr[:HALF] = ord_lo[...]
    x_scr[HALF:] = ord_hi[...]

    vt[...] = jnp.full((H, 2 * D, N), VSCALE, bf16)
    for b in range(N // ROWS):
        sl = slice(b * ROWS, (b + 1) * ROWS)
        unit, _ = normalize(x_scr[sl].astype(f32))
        normed = (unit * gain1[...]).astype(bf16)
        qkv = dg(normed, wqkv[...], 1, 0).astype(bf16)
        kn[0, sl] = qkv[:, 256:384]
        kn[1, sl] = qkv[:, 384:512]
        vn[0, sl] = qkv[:, 512:640]
        vn[1, sl] = qkv[:, 640:768]
        flipped = jnp.transpose(qkv)
        qt[:, sl] = flipped[:256]
        kt[:, sl] = flipped[256:512]
        vt[:, :D, sl] = flipped[512:].reshape(H, D, ROWS) * bf16(VSCALE)

    lane_head = lax.broadcasted_iota(jnp.int32, (N, 128), 1) // D

    def forward_head(h, carry):
        block = h // 8
        mask = lane_head == h % 8
        keys = jnp.where(mask, kn[block], bf16(0))
        scores = dg(keys, qt[pl.ds(block * 128, 128)], 1, 0)
        weights = jnp.exp2(scores * SCORE).astype(bf16)
        e_scr[h] = weights
        sums = dg(vt[h], weights, 1, 0)
        total = sums[D : D + 1]
        amp = jnp.where(total >= 2.0**40, 2.0**-80, jnp.where(total < 2.0**-40, 2.0**80, 1.0))
        inverse = 1.0 / (total * amp)
        ot[pl.ds(h * D, D)] = (sums[:D] * amp) * inverse
        inv_scr[pl.ds(h * D, D)] = jnp.broadcast_to(inverse * VSCALE, (D, N))
        amp_scr[h] = jnp.broadcast_to(amp, (D, N)).astype(bf16)
        return carry

    lax.fori_loop(0, H, forward_head, 0)

    for b in range(N // ROWS):
        sl = slice(b * ROWS, (b + 1) * ROWS)
        half = b // 2
        hs = slice((b % 2) * ROWS, (b % 2 + 1) * ROWS)
        attention = jnp.transpose(ot[:, sl].astype(bf16))
        mixed = x_scr[sl].astype(f32) + dg(attention, wproj[...], 1, 0)
        unit, scale = normalize(mixed)
        normed = (unit * gain2[...]).astype(bf16)
        pre = dg(normed, wfc1[...], 1, 0)
        cdf = 0.5 * (1.0 + lax.erf(pre * (2.0**-0.5)))
        act = (pre * cdf).astype(bf16)
        (out_lo, out_hi)[half][hs] = (mixed + dg(act, wfc2[...], 1, 0)).astype(bf16)
        cot = (cot_lo, cot_hi)[half][hs]
        grad_act = dg(cot, wfc2[...], 1, 1)
        density = jnp.exp(-0.5 * pre * pre) * (1.0 / math.sqrt(2.0 * math.pi))
        grad_pre = (grad_act * (cdf + pre * density)).astype(bf16)
        grad_normed = dg(grad_pre, wfc1[...], 1, 1)
        grad_mixed = cot.astype(f32) + normalize_back(grad_normed * gain2[...], unit, scale)
        mix_grad[sl] = grad_mixed
        grad_att = dg(grad_mixed.astype(bf16), wproj[...], 1, 1).astype(bf16)
        gt[:, sl] = (jnp.transpose(grad_att).astype(f32) * inv_scr[:, sl]).astype(bf16)

    def backward_head(h, carry):
        block = h // 8
        rows = pl.ds(h * D, D)
        mask = lane_head == h % 8
        values = jnp.where(mask, vn[block], bf16(0))
        grads = gt[rows]
        inner = jnp.sum(grads.astype(f32) * ot[rows], axis=0, keepdims=True)
        probs = e_scr[h] * amp_scr[h, :1]
        dt[pl.ds(512 + h * D, D)] = dg(grads, probs, 1, 1).astype(bf16)
        grad_probs = dg(values, gt[pl.ds(block * 128, 128)], 1, 0) - inner
        grad_scores = probs * grad_probs.astype(bf16)
        dt[rows] = (dg(kt[rows], grad_scores, 1, 0) * 0.25).astype(bf16)
        dt[pl.ds(256 + h * D, D)] = (dg(qt[rows], grad_scores, 1, 1) * 0.25).astype(bf16)
        return carry

    lax.fori_loop(0, H, backward_head, 0)

    for b in range(N // ROWS):
        sl = slice(b * ROWS, (b + 1) * ROWS)
        half = b // 2
        hs = slice((b % 2) * ROWS, (b % 2 + 1) * ROWS)
        grad_qkv = jnp.transpose(dt[:, sl])
        grad_normed = dg(grad_qkv, wqkv[...], 1, 1)
        unit, scale = normalize(x_scr[sl].astype(f32))
        grad = mix_grad[sl] + normalize_back(grad_normed * gain1[...], unit, scale)
        (grad_lo, grad_hi)[half][hs] = grad.astype(bf16)


PARAMS = pltpu.CompilerParams(vmem_limit_bytes=60 * 1024 * 1024)


def call(kernel, outs, scratch=(), name=None):
    return pl.pallas_call(
        kernel,
        out_shape=tuple(jax.ShapeDtypeStruct(s, bf16) for s in outs),
        scratch_shapes=list(scratch),
        compiler_params=PARAMS,
        name=name,
    )


def shift(rows, step):
    axes = ("gx", "gy")
    count = lax.axis_size(axes)
    return lax.ppermute(rows, axes, [(i, (i + step) % count) for i in range(count)])


def shards(
    points, send_rows, recv_slot, norm1_gain, qkv_weight, proj_weight, norm2_gain,
    fc1_weight, fc2_weight, cotangent,
):
    local = points[0]
    sender = send_rows[0]
    slot = recv_slot
    cot = cotangent[0]
    gain1 = norm1_gain.reshape(1, C)
    gain2 = norm2_gain.reshape(1, C)

    left, right = call(gather_kernel, [(CAP, C)] * 2, name="gather")(local, sender)
    from_prev = shift(right, 1)
    from_next = shift(left, -1)
    cot_lo = shift(cot[HALF:], 1)
    first, second = call(order_kernel, [(HALF, C)] * 2, name="order")(
        local, from_prev, from_next, slot
    )
    ord_lo = shift(second, 1)
    vm = pltpu.VMEM
    out_lo, out_hi, grad_lo, grad_hi = call(
        main_kernel,
        [(HALF, C)] * 4,
        [
            vm((H, N, N), bf16),
            vm((N, C), bf16),
            vm((2, N, 128), bf16),
            vm((2, N, 128), bf16),
            vm((C, N), bf16),
            vm((C, N), bf16),
            vm((H, 2 * D, N), bf16),
            vm((C, N), f32),
            vm((C, N), f32),
            vm((H, D, N), bf16),
            vm((C, N), bf16),
            vm((N, C), f32),
            vm((3 * C, N), bf16),
        ],
        name="block",
    )(
        ord_lo, first, cot_lo, cot[:HALF], gain1, qkv_weight, proj_weight, gain2,
        fc1_weight, fc2_weight,
    )
    grad_second = shift(grad_lo, -1)
    out_second = shift(out_lo, -1)
    to_prev, to_next = call(back_kernel, [(CAP, C)] * 2, name="back")(grad_hi, grad_second, slot)
    back_left = shift(to_prev, -1)
    back_right = shift(to_next, 1)
    (own,) = call(own_kernel, [(N, C)], name="own")(grad_hi, grad_second, slot)
    (grad_points,) = call(final_kernel, [(N, C)], name="final")(own, back_right, back_left, sender)
    block_out = jnp.concatenate([out_hi, out_second], axis=0)
    return (block_out[None], grad_points[None])


def solution(mesh):
    rows = P(None, ("gx", "gy"), None)
    in_specs = (rows, rows, P(None, ("gx", "gy")), P(), P(), P(), P(), P(), P(), rows)
    return jax.shard_map(
        shards, mesh=mesh, in_specs=in_specs, out_specs=(rows, rows), check_vma=False
    )
```

```python
import functools
import math

import jax
import jax.numpy as jnp
from jax import lax
from jax.experimental import pallas as pl
from jax.experimental.pallas import tpu as pltpu
from jax.sharding import PartitionSpec as P

H = 16
D = 16
C = 256
N = 1024
HALF = 512
CAP = 384
FF = 1024
ROWS = 256
EPS = 1e-05
LOG2E = 1.4426950408889634
SCORE = LOG2E / 4.0
VSCALE = 2.0**-8

bf16 = jnp.bfloat16
f32 = jnp.float32


def dg(a, b, ca, cb):
    return lax.dot_general(a, b, (((ca,), (cb,)), ((), ())), preferred_element_type=f32)


def column(row, count):
    return jnp.transpose(jnp.broadcast_to(row, (128, count)))


def picks_from_column(col, start, width):
    lanes = lax.broadcasted_iota(jnp.int32, col.shape, 1)
    parts = [
        jnp.where(col == lanes + (start + 128 * b), 1.0, 0.0).astype(bf16)
        for b in range(width // 128)
    ]
    return jnp.concatenate(parts, axis=1)


def picks_from_row(row, start, height):
    ids = lax.broadcasted_iota(jnp.int32, (height, row.shape[1]), 0) + start
    return jnp.where(ids == row, 1.0, 0.0).astype(bf16)


class Fetch:
    def __init__(self, pairs, sems):
        self.copies = [
            pltpu.make_async_copy(src, dst, sems.at[i]) for i, (src, dst) in enumerate(pairs)
        ]
        for copy in self.copies:
            copy.start()

    def wait(self, *which):
        for i in which:
            self.copies[i].wait()


def gather_kernel(points, sender, left, right, points_v, rows_v, sems):
    fetch = Fetch([(points, points_v)], sems)
    picks = picks_from_column(column(sender[...], 2 * CAP), 0, N)
    fetch.wait(0)
    rows_v[:CAP] = dg(picks[:CAP], points_v[...], 1, 0).astype(bf16)
    store = pltpu.make_async_copy(rows_v.at[:CAP], left, sems.at[1])
    store.start()
    rows_v[CAP:] = dg(picks[CAP:], points_v[...], 1, 0).astype(bf16)
    last = pltpu.make_async_copy(rows_v.at[CAP:], right, sems.at[2])
    last.start()
    store.wait()
    last.wait()


def order_kernel(points, from_prev, from_next, slot, first, second, pool, rows_v, sems):
    fetch = Fetch(
        [
            (points, pool.at[:N]),
            (from_prev, pool.at[N : N + CAP]),
            (from_next, pool.at[N + CAP :]),
        ],
        sems,
    )
    picks = picks_from_column(column(slot[...], N), 0, N + 2 * CAP)
    fetch.wait(0, 1, 2)
    rows_v[HALF:] = dg(picks[HALF:], pool[...], 1, 0).astype(bf16)
    store = pltpu.make_async_copy(rows_v.at[HALF:], second, sems.at[3])
    store.start()
    rows_v[:HALF] = dg(picks[:HALF], pool[...], 1, 0).astype(bf16)
    last = pltpu.make_async_copy(rows_v.at[:HALF], first, sems.at[4])
    last.start()
    store.wait()
    last.wait()


def back_kernel(first, second, slot, to_prev, to_next, grads, rows_v, sems):
    fetch = Fetch([(first, grads.at[:HALF]), (second, grads.at[HALF:])], sems)
    picks = picks_from_row(slot[...], N, 2 * CAP)
    fetch.wait(0, 1)
    rows_v[:CAP] = dg(picks[:CAP], grads[...], 1, 0).astype(bf16)
    store = pltpu.make_async_copy(rows_v.at[:CAP], to_prev, sems.at[2])
    store.start()
    rows_v[CAP:] = dg(picks[CAP:], grads[...], 1, 0).astype(bf16)
    last = pltpu.make_async_copy(rows_v.at[CAP:], to_next, sems.at[3])
    last.start()
    store.wait()
    last.wait()


def own_kernel(first, second, slot, out, grads, rows_v, sems):
    fetch = Fetch([(first, grads.at[:HALF]), (second, grads.at[HALF:])], sems)
    picks = picks_from_row(slot[...], 0, N)
    fetch.wait(0, 1)
    rows_v[...] = dg(picks, grads[...], 1, 0).astype(bf16)
    pltpu.sync_copy(rows_v, out)


def final_kernel(own, left, right, sender, out, own_v, returned, rows_v, sems):
    fetch = Fetch(
        [(left, returned.at[:CAP]), (right, returned.at[CAP:]), (own, own_v)], sems
    )
    picks = picks_from_row(sender[...], 0, N)
    fetch.wait(0, 1, 2)
    stores = []
    for b in range(2):
        sl = slice(b * HALF, (b + 1) * HALF)
        rows = dg(picks[sl], returned[...], 1, 0)
        rows_v[sl] = (own_v[sl].astype(f32) + rows).astype(bf16)
        stores.append(pltpu.make_async_copy(rows_v.at[sl], out.at[sl], sems.at[3 + b]))
        stores[-1].start()
    for store in stores:
        store.wait()


def normalize(rows):
    mean = jnp.mean(rows, axis=-1, keepdims=True)
    centered = rows - mean
    spread = jnp.mean(centered * centered, axis=-1, keepdims=True)
    scale = lax.rsqrt(spread + EPS)
    return centered * scale, scale


def normalize_back(grad, unit, scale):
    return scale * (
        grad
        - jnp.mean(grad, axis=-1, keepdims=True)
        - unit * jnp.mean(grad * unit, axis=-1, keepdims=True)
    )


def main_kernel(
    ord_lo, ord_hi, cot_lo, cot_hi, wqkv_h, wproj_h, wfc1_h, wfc2_h, gain1, gain2,
    out_lo, out_hi, grad_lo, grad_hi,
    wqkv, wproj, wfc1, wfc2, cot_v, out_v, probs_t, scores_t, sems,
    e_scr, x_scr, kn, vn, qt, kt, vt, ot, inv_scr, amp_scr, gt, mix_grad, dt,
):
    fetch = Fetch(
        [
            (ord_hi, x_scr.at[HALF:]),
            (wqkv_h, wqkv),
            (ord_lo, x_scr.at[:HALF]),
            (wproj_h, wproj),
            (wfc1_h, wfc1),
            (wfc2_h, wfc2),
            (cot_lo, cot_v.at[:HALF]),
            (cot_hi, cot_v.at[HALF:]),
        ],
        sems,
    )
    vt[...] = jnp.full((H, 2 * D, N), VSCALE, bf16)
    fetch.wait(0, 1, 2)
    for b in range(N // ROWS):
        sl = slice(b * ROWS, (b + 1) * ROWS)
        unit, _ = normalize(x_scr[sl].astype(f32))
        normed = (unit * gain1[...]).astype(bf16)
        qkv = dg(normed, wqkv[...], 1, 0).astype(bf16)
        kn[0, sl] = qkv[:, 256:384]
        kn[1, sl] = qkv[:, 384:512]
        vn[0, sl] = qkv[:, 512:640]
        vn[1, sl] = qkv[:, 640:768]
        flipped = jnp.transpose(qkv)
        qt[:, sl] = flipped[:256]
        kt[:, sl] = flipped[256:512]
        vt[:, :D, sl] = flipped[512:].reshape(H, D, ROWS) * bf16(VSCALE)

    lane_head = lax.broadcasted_iota(jnp.int32, (N, 128), 1) // D

    def forward_head(h, carry):
        block = h // 8
        mask = lane_head == h % 8
        keys = jnp.where(mask, kn[block], bf16(0))
        scores = dg(keys, qt[pl.ds(block * 128, 128)], 1, 0)
        weights = jnp.exp2(scores * SCORE).astype(bf16)
        e_scr[h] = weights
        sums = dg(vt[h], weights, 1, 0)
        total = sums[D : D + 1]
        amp = jnp.where(total >= 2.0**40, 2.0**-80, jnp.where(total < 2.0**-40, 2.0**80, 1.0))
        inverse = 1.0 / (total * amp)
        ot[pl.ds(h * D, D)] = (sums[:D] * amp) * inverse
        inv_scr[pl.ds(h * D, D)] = jnp.broadcast_to(inverse * VSCALE, (D, N))
        amp_scr[h] = jnp.broadcast_to(amp, (D, N)).astype(bf16)
        return carry

    lax.fori_loop(0, H, forward_head, 0)
    fetch.wait(3, 4, 5, 6, 7)

    for b in range(N // ROWS):
        sl = slice(b * ROWS, (b + 1) * ROWS)
        attention = jnp.transpose(ot[:, sl].astype(bf16))
        mixed = x_scr[sl].astype(f32) + dg(attention, wproj[...], 1, 0)
        unit, scale = normalize(mixed)
        normed = (unit * gain2[...]).astype(bf16)
        pre = dg(normed, wfc1[...], 1, 0)
        cdf = 0.5 * (1.0 + lax.erf(pre * (2.0**-0.5)))
        act = (pre * cdf).astype(bf16)
        out_v[sl] = (mixed + dg(act, wfc2[...], 1, 0)).astype(bf16)
        cot = cot_v[sl]
        grad_act = dg(cot, wfc2[...], 1, 1)
        density = jnp.exp(-0.5 * pre * pre) * (1.0 / math.sqrt(2.0 * math.pi))
        grad_pre = (grad_act * (cdf + pre * density)).astype(bf16)
        grad_normed = dg(grad_pre, wfc1[...], 1, 1)
        grad_mixed = cot.astype(f32) + normalize_back(grad_normed * gain2[...], unit, scale)
        mix_grad[sl] = grad_mixed
        grad_att = dg(grad_mixed.astype(bf16), wproj[...], 1, 1).astype(bf16)
        gt[:, sl] = (jnp.transpose(grad_att).astype(f32) * inv_scr[:, sl]).astype(bf16)

    stores = [
        pltpu.make_async_copy(out_v.at[:HALF], out_lo, sems.at[8]),
        pltpu.make_async_copy(out_v.at[HALF:], out_hi, sems.at[9]),
    ]
    for store in stores:
        store.start()

    def backward_head(h, carry):
        block = h // 8
        rows = pl.ds(h * D, D)
        mask = lane_head == h % 8
        values = jnp.where(mask, vn[block], bf16(0))
        grads = gt[rows]
        inner = jnp.sum(grads.astype(f32) * ot[rows], axis=0, keepdims=True)
        probs = e_scr[h] * amp_scr[h, :1]
        probs_t[...] = jnp.transpose(probs)
        grad_probs = dg(values, gt[pl.ds(block * 128, 128)], 1, 0) - inner
        grad_scores = probs * grad_probs.astype(bf16)
        dt[rows] = (dg(kt[rows], grad_scores, 1, 0) * 0.25).astype(bf16)
        dt[pl.ds(512 + h * D, D)] = dg(grads, probs_t[...], 1, 0).astype(bf16)
        scores_t[...] = jnp.transpose(grad_scores)
        dt[pl.ds(256 + h * D, D)] = (dg(qt[rows], scores_t[...], 1, 0) * 0.25).astype(bf16)
        return carry

    lax.fori_loop(0, H, backward_head, 0)
    for store in stores:
        store.wait()

    for b in range(N // ROWS):
        sl = slice(b * ROWS, (b + 1) * ROWS)
        grad_qkv = jnp.transpose(dt[:, sl])
        grad_normed = dg(grad_qkv, wqkv[...], 1, 1)
        unit, scale = normalize(x_scr[sl].astype(f32))
        grad = mix_grad[sl] + normalize_back(grad_normed * gain1[...], unit, scale)
        out_v[sl] = grad.astype(bf16)
        if b % 2:
            hs = slice((b // 2) * HALF, (b // 2 + 1) * HALF)
            out = (grad_lo, grad_hi)[b // 2]
            stores[b // 2] = pltpu.make_async_copy(out_v.at[hs], out, sems.at[10 + b // 2])
            stores[b // 2].start()
    for store in stores:
        store.wait()


PARAMS = pltpu.CompilerParams(vmem_limit_bytes=60 * 1024 * 1024)
vm = pltpu.VMEM


def call(kernel, anys, others, outs, scratch, sems, name):
    anyspace = pl.BlockSpec(memory_space=pl.ANY)
    vmspace = pl.BlockSpec(memory_space=pltpu.VMEM)
    return pl.pallas_call(
        kernel,
        in_specs=[anyspace] * len(anys) + [vmspace] * len(others),
        out_specs=tuple([anyspace] * len(outs)),
        out_shape=tuple(jax.ShapeDtypeStruct(s, bf16) for s in outs),
        scratch_shapes=list(scratch) + ([pltpu.SemaphoreType.DMA((sems,))] if sems else []),
        compiler_params=PARAMS,
        name=name,
    )(*anys, *others)


def shift(rows, step):
    axes = ("gx", "gy")
    count = lax.axis_size(axes)
    return lax.ppermute(rows, axes, [(i, (i + step) % count) for i in range(count)])


def shards(
    points, send_rows, recv_slot, norm1_gain, qkv_weight, proj_weight, norm2_gain,
    fc1_weight, fc2_weight, cotangent,
):
    local = points[0]
    sender = send_rows[0]
    slot = recv_slot
    cot = cotangent[0]
    gain1 = norm1_gain.reshape(1, C)
    gain2 = norm2_gain.reshape(1, C)

    block = vm((N, C), bf16)
    slots = vm((2 * CAP, C), bf16)
    left, right = call(
        gather_kernel, [local], [sender], [(CAP, C)] * 2, [block, slots], 3, "gather"
    )
    from_prev = shift(right, 1)
    from_next = shift(left, -1)
    cot_lo = shift(cot[HALF:], 1)
    first, second = call(
        order_kernel,
        [local, from_prev, from_next],
        [slot],
        [(HALF, C)] * 2,
        [vm((N + 2 * CAP, C), bf16), block],
        5,
        "order",
    )
    ord_lo = shift(second, 1)
    out_lo, out_hi, grad_lo, grad_hi = call(
        main_kernel,
        [ord_lo, first, cot_lo, cot[:HALF], qkv_weight, proj_weight, fc1_weight, fc2_weight],
        [gain1, gain2],
        [(HALF, C)] * 4,
        [
            vm((C, 3 * C), bf16),
            vm((C, C), bf16),
            vm((C, FF), bf16),
            vm((FF, C), bf16),
            block,
            block,
            vm((N, N), bf16),
            vm((N, N), bf16),
            pltpu.SemaphoreType.DMA((12,)),
            vm((H, N, N), bf16),
            block,
            vm((2, N, 128), bf16),
            vm((2, N, 128), bf16),
            vm((C, N), bf16),
            vm((C, N), bf16),
            vm((H, 2 * D, N), bf16),
            vm((C, N), f32),
            vm((C, N), f32),
            vm((H, D, N), bf16),
            vm((C, N), bf16),
            vm((N, C), f32),
            vm((3 * C, N), bf16),
        ],
        0,
        "block",
    )
    grad_second = shift(grad_lo, -1)
    out_second = shift(out_lo, -1)
    to_prev, to_next = call(
        back_kernel, [grad_hi, grad_second], [slot], [(CAP, C)] * 2, [block, slots], 4, "back"
    )
    back_left = shift(to_prev, -1)
    back_right = shift(to_next, 1)
    (own,) = call(own_kernel, [grad_hi, grad_second], [slot], [(N, C)], [block, block], 2, "own")
    (grad_points,) = call(
        final_kernel,
        [own, back_right, back_left],
        [sender],
        [(N, C)],
        [block, slots, block],
        5,
        "final",
    )
    block_out = jnp.concatenate([out_hi, out_second], axis=0)
    return (block_out[None], grad_points[None])


def solution(mesh):
    rows = P(None, ("gx", "gy"), None)
    in_specs = (rows, rows, P(None, ("gx", "gy")), P(), P(), P(), P(), P(), P(), rows)
    return jax.shard_map(
        shards, mesh=mesh, in_specs=in_specs, out_specs=(rows, rows), check_vma=False
    )
```

```python
import functools
import math

import jax
import jax.numpy as jnp
from jax import lax
from jax.experimental import pallas as pl
from jax.experimental.pallas import tpu as pltpu
from jax.sharding import PartitionSpec as P

H = 16
D = 16
C = 256
N = 1024
HALF = 512
CAP = 384
FF = 1024
ROWS = 256
EPS = 1e-05
LOG2E = 1.4426950408889634
SCORE = LOG2E / 4.0
VSCALE = 2.0**-8

bf16 = jnp.bfloat16
f32 = jnp.float32


def dg(a, b, ca, cb):
    return lax.dot_general(a, b, (((ca,), (cb,)), ((), ())), preferred_element_type=f32)


def column(row, count):
    return jnp.transpose(jnp.broadcast_to(row, (128, count)))


def picks_from_column(col, start, width):
    lanes = lax.broadcasted_iota(jnp.int32, col.shape, 1)
    parts = [
        jnp.where(col == lanes + (start + 128 * b), 1.0, 0.0).astype(bf16)
        for b in range(width // 128)
    ]
    return jnp.concatenate(parts, axis=1)


def picks_from_row(row, start, height):
    ids = lax.broadcasted_iota(jnp.int32, (height, row.shape[1]), 0) + start
    return jnp.where(ids == row, 1.0, 0.0).astype(bf16)


def gather_kernel(points, sender, left, right):
    col = column(sender[...], 2 * CAP)
    rows = dg(picks_from_column(col, 0, N), points[...], 1, 0).astype(bf16)
    left[...] = rows[:CAP]
    right[...] = rows[CAP:]


def order_kernel(points, from_prev, from_next, slot, first, second):
    col = column(slot[...], N)
    rows = dg(picks_from_column(col, 0, N), points[...], 1, 0)
    rows += dg(picks_from_column(col, N, CAP), from_prev[...], 1, 0)
    rows += dg(picks_from_column(col, N + CAP, CAP), from_next[...], 1, 0)
    rows = rows.astype(bf16)
    first[...] = rows[:HALF]
    second[...] = rows[HALF:]


def back_kernel(first, second, slot, to_prev, to_next):
    row = slot[...]
    picks = picks_from_row(row, N, 2 * CAP)
    rows = dg(picks[:, :HALF], first[...], 1, 0) + dg(picks[:, HALF:], second[...], 1, 0)
    rows = rows.astype(bf16)
    to_prev[...] = rows[:CAP]
    to_next[...] = rows[CAP:]


def own_kernel(first, second, slot, out):
    picks = picks_from_row(slot[...], 0, N)
    rows = dg(picks[:, :HALF], first[...], 1, 0) + dg(picks[:, HALF:], second[...], 1, 0)
    out[...] = rows.astype(bf16)


def final_kernel(own, left, right, sender, out):
    picks = picks_from_row(sender[...], 0, N)
    rows = dg(picks[:, :CAP], left[...], 1, 0) + dg(picks[:, CAP:], right[...], 1, 0)
    out[...] = (own[...].astype(f32) + rows).astype(bf16)


def normalize(rows):
    mean = jnp.mean(rows, axis=-1, keepdims=True)
    centered = rows - mean
    spread = jnp.mean(centered * centered, axis=-1, keepdims=True)
    scale = lax.rsqrt(spread + EPS)
    return centered * scale, scale


def normalize_back(grad, unit, scale):
    return scale * (
        grad
        - jnp.mean(grad, axis=-1, keepdims=True)
        - unit * jnp.mean(grad * unit, axis=-1, keepdims=True)
    )


def front(rows, gain, weight):
    unit, _ = normalize(rows.astype(f32))
    return dg((unit * gain).astype(bf16), weight, 1, 0).astype(bf16)


def split_qkv(rows_ref, gain, weight, kn, vn, qt, kt, vt):
    vt[...] = jnp.full(vt.shape, VSCALE, bf16)
    for b in range(HALF // ROWS):
        sl = slice(b * ROWS, (b + 1) * ROWS)
        qkv = front(rows_ref[sl], gain[...], weight[...])
        kn[0, sl] = qkv[:, 256:384]
        kn[1, sl] = qkv[:, 384:512]
        vn[0, sl] = qkv[:, 512:640]
        vn[1, sl] = qkv[:, 640:768]
        flipped = jnp.transpose(qkv)
        qt[:, sl] = flipped[:256]
        kt[:, sl] = flipped[256:512]
        vt[:, :D, sl] = flipped[512:].reshape(H, D, ROWS) * bf16(VSCALE)


def front_back(dt, rows_ref, mix_grad, gain, weight, out):
    for b in range(HALF // ROWS):
        sl = slice(b * ROWS, (b + 1) * ROWS)
        grad_normed = dg(jnp.transpose(dt[:, sl]), weight[...], 1, 1)
        unit, scale = normalize(rows_ref[sl].astype(f32))
        grad = mix_grad[sl] + normalize_back(grad_normed * gain[...], unit, scale)
        out[sl] = grad.astype(bf16)


def head_mask(h):
    return lax.broadcasted_iota(jnp.int32, (HALF, 128), 1) // D == h % 8


def weigh(keys, queries):
    return jnp.exp2(dg(keys, queries, 1, 0) * SCORE).astype(bf16)


def before_kernel(ord_hi, wqkv, gain1, kn, vn, qt, kt, vt, e_hh, sums_hh):
    split_qkv(ord_hi, gain1, wqkv, kn, vn, qt, kt, vt)

    def one_head(h, carry):
        block = h // 8
        keys = jnp.where(head_mask(h), kn[block], bf16(0))
        weights = weigh(keys, qt[pl.ds(block * 128, 128)])
        e_hh[h] = weights
        sums_hh[h] = dg(vt[h], weights, 1, 0)
        return carry

    lax.fori_loop(0, H, one_head, 0)


def main_kernel(
    ord_lo, ord_hi, cot_lo, cot_hi, wqkv, wproj, wfc1, wfc2, gain1, gain2,
    kn_hi, vn_hi, qt_hi, kt_hi, vt_hi, sums_hh,
    out_lo, out_hi, grad_lo, gt_hi, inner_hi, amp_hi, part, mix_hi,
    e_l, e_hl, kn, vn, qt, kt, vt, ot, inv_scr, amp_scr, gt, mix_lo, dt, p_t, s_t, ph_t, sh_t,
):
    split_qkv(ord_lo, gain1, wqkv, kn, vn, qt.at[:, :HALF], kt, vt)
    qt[:, HALF:] = qt_hi[...]

    def forward_head(h, carry):
        block = h // 8
        mask = head_mask(h)
        lanes = pl.ds(block * 128, 128)
        weights = weigh(jnp.where(mask, kn[block], bf16(0)), qt[lanes])
        e_l[h] = weights
        side = weigh(jnp.where(mask, kn_hi[block], bf16(0)), qt[lanes, :HALF])
        e_hl[h] = side
        sums = dg(vt[h], weights, 1, 0)
        sums += jnp.concatenate([dg(vt_hi[h], side, 1, 0), sums_hh[h]], axis=1)
        total = sums[D : D + 1]
        amp = jnp.where(total >= 2.0**40, 2.0**-80, jnp.where(total < 2.0**-40, 2.0**80, 1.0))
        inverse = 1.0 / (total * amp)
        ot[pl.ds(h * D, D)] = (sums[:D] * amp) * inverse
        inv_scr[pl.ds(h * D, D)] = jnp.broadcast_to(inverse * VSCALE, (D, N))
        amp_scr[h] = jnp.broadcast_to(amp, (D, N)).astype(bf16)
        return carry

    lax.fori_loop(0, H, forward_head, 0)

    for b in range(N // ROWS):
        sl = slice(b * ROWS, (b + 1) * ROWS)
        half = b // 2
        hs = slice((b % 2) * ROWS, (b % 2 + 1) * ROWS)
        attention = jnp.transpose(ot[:, sl].astype(bf16))
        mixed = (ord_lo, ord_hi)[half][hs].astype(f32) + dg(attention, wproj[...], 1, 0)
        unit, scale = normalize(mixed)
        normed = (unit * gain2[...]).astype(bf16)
        pre = dg(normed, wfc1[...], 1, 0)
        cdf = 0.5 * (1.0 + lax.erf(pre * (2.0**-0.5)))
        act = (pre * cdf).astype(bf16)
        (out_lo, out_hi)[half][hs] = (mixed + dg(act, wfc2[...], 1, 0)).astype(bf16)
        cot = (cot_lo, cot_hi)[half][hs]
        grad_act = dg(cot, wfc2[...], 1, 1)
        density = jnp.exp(-0.5 * pre * pre) * (1.0 / math.sqrt(2.0 * math.pi))
        grad_pre = (grad_act * (cdf + pre * density)).astype(bf16)
        grad_normed = dg(grad_pre, wfc1[...], 1, 1)
        grad_mixed = cot.astype(f32) + normalize_back(grad_normed * gain2[...], unit, scale)
        (mix_lo, mix_hi)[half][hs] = grad_mixed
        grad_att = dg(grad_mixed.astype(bf16), wproj[...], 1, 1).astype(bf16)
        gt[:, sl] = (jnp.transpose(grad_att).astype(f32) * inv_scr[:, sl]).astype(bf16)

    gt_hi[...] = gt[:, HALF:]
    amp_hi[...] = amp_scr[:, :, HALF:]

    def backward_head(h, carry):
        block = h // 8
        rows = pl.ds(h * D, D)
        rows_k = pl.ds(256 + h * D, D)
        rows_v = pl.ds(512 + h * D, D)
        lanes = pl.ds(block * 128, 128)
        mask = head_mask(h)
        grads = gt[rows]
        inner = jnp.sum(grads.astype(f32) * ot[rows], axis=0, keepdims=True)
        inner_hi[h] = jnp.broadcast_to(inner[:, HALF:], (8, HALF))
        amp = amp_scr[h, :1]
        probs = e_l[h] * amp
        p_t[...] = jnp.transpose(probs)
        side = e_hl[h] * amp[:, :HALF]
        ph_t[...] = jnp.transpose(side)
        values = jnp.where(mask, vn[block], bf16(0))
        scores = probs * (dg(values, gt[lanes], 1, 0) - inner).astype(bf16)
        grad_q = dg(kt[rows], scores, 1, 0)
        values = jnp.where(mask, vn_hi[block], bf16(0))
        side_scores = side * (dg(values, gt[lanes, :HALF], 1, 0) - inner[:, :HALF]).astype(bf16)
        s_t[...] = jnp.transpose(scores)
        sh_t[...] = jnp.transpose(side_scores)
        dt[rows] = ((grad_q[:, :HALF] + dg(kt_hi[rows], side_scores, 1, 0)) * 0.25).astype(bf16)
        part[rows] = grad_q[:, HALF:]
        dt[rows_v] = dg(grads, p_t[...], 1, 0).astype(bf16)
        part[rows_v] = dg(gt[rows, :HALF], ph_t[...], 1, 0)
        dt[rows_k] = (dg(qt[rows], s_t[...], 1, 0) * 0.25).astype(bf16)
        part[rows_k] = dg(qt[rows, :HALF], sh_t[...], 1, 0)
        return carry

    lax.fori_loop(0, H, backward_head, 0)
    front_back(dt, ord_lo, mix_lo, gain1, wqkv, grad_lo)


def after_kernel(
    ord_hi, wqkv, gain1, vn, qt, kt, e_hh, gt, inner_hi, amp_hi, part, mix_hi,
    grad_hi, dt, p_t, s_t,
):
    def backward_head(h, carry):
        block = h // 8
        rows = pl.ds(h * D, D)
        rows_k = pl.ds(256 + h * D, D)
        rows_v = pl.ds(512 + h * D, D)
        probs = e_hh[h] * amp_hi[h, :1]
        p_t[...] = jnp.transpose(probs)
        values = jnp.where(head_mask(h), vn[block], bf16(0))
        inner = inner_hi[h][:1]
        scores = probs * (dg(values, gt[pl.ds(block * 128, 128)], 1, 0) - inner).astype(bf16)
        s_t[...] = jnp.transpose(scores)
        dt[rows] = ((part[rows] + dg(kt[rows], scores, 1, 0)) * 0.25).astype(bf16)
        dt[rows_v] = (part[rows_v] + dg(gt[rows], p_t[...], 1, 0)).astype(bf16)
        dt[rows_k] = ((part[rows_k] + dg(qt[rows], s_t[...], 1, 0)) * 0.25).astype(bf16)
        return carry

    lax.fori_loop(0, H, backward_head, 0)
    front_back(dt, ord_hi, mix_hi, gain1, wqkv, grad_hi)


vm = pltpu.VMEM


def chip(rows):
    return pltpu.with_memory_space_constraint(rows, pltpu.VMEM)


def call(kernel, operands, outs, scratch, name, limit=16):
    space = pl.BlockSpec(memory_space=pltpu.VMEM)
    return pl.pallas_call(
        kernel,
        in_specs=[space] * len(operands),
        out_specs=tuple([space] * len(outs)),
        out_shape=tuple(
            o if not isinstance(o, tuple) else jax.ShapeDtypeStruct(o, bf16) for o in outs
        ),
        scratch_shapes=list(scratch),
        compiler_params=pltpu.CompilerParams(vmem_limit_bytes=limit << 20),
        name=name,
    )(*operands)


def shift(rows, step):
    axes = ("gx", "gy")
    count = lax.axis_size(axes)
    return lax.ppermute(rows, axes, [(i, (i + step) % count) for i in range(count)])


def shards(
    points, send_rows, recv_slot, norm1_gain, qkv_weight, proj_weight, norm2_gain,
    fc1_weight, fc2_weight, cotangent,
):
    local = points[0]
    sender = send_rows[0]
    slot = recv_slot
    cot = cotangent[0]
    gain1 = norm1_gain.reshape(1, C)
    gain2 = norm2_gain.reshape(1, C)

    left, right = call(gather_kernel, [local, sender], [(CAP, C)] * 2, [], "gather")
    from_prev = shift(right, 1)
    from_next = shift(left, -1)
    cot_lo = shift(cot[HALF:], 1)
    ord_hi, second = call(
        order_kernel,
        [local, chip(from_prev), chip(from_next), slot],
        [(HALF, C)] * 2,
        [],
        "order",
    )
    ord_lo = shift(second, 1)
    natural = vm((2, HALF, 128), bf16)
    flipped = vm((C, HALF), bf16)
    valued = vm((H, 2 * D, HALF), bf16)
    square = vm((H, HALF, HALF), bf16)
    kn, vn, qt, kt, vt, e_hh, sums_hh = call(
        before_kernel,
        [ord_hi, qkv_weight, gain1],
        [natural, natural, flipped, flipped, valued, square, vm((H, 2 * D, HALF), f32)],
        [],
        "before",
        24,
    )
    out_lo, out_hi, grad_lo, gt_hi, inner_hi, amp_hi, part, mix_hi = call(
        main_kernel,
        [
            chip(ord_lo), ord_hi, chip(cot_lo), cot[:HALF], qkv_weight, proj_weight,
            fc1_weight, fc2_weight, gain1, gain2, kn, vn, qt, kt, vt, sums_hh,
        ],
        [
            (HALF, C), (HALF, C), (HALF, C), flipped, vm((H, 8, HALF), f32),
            vm((H, D, HALF), bf16), vm((3 * C, HALF), f32), vm((HALF, C), f32),
        ],
        [
            vm((H, HALF, N), bf16), square, natural, natural, vm((C, N), bf16), flipped, valued,
            vm((C, N), f32), vm((C, N), f32), vm((H, D, N), bf16), vm((C, N), bf16),
            vm((HALF, C), f32), vm((3 * C, HALF), bf16), vm((N, HALF), bf16),
            vm((N, HALF), bf16), vm((HALF, HALF), bf16), vm((HALF, HALF), bf16),
        ],
        "block",
        40,
    )
    grad_second = shift(grad_lo, -1)
    out_second = shift(out_lo, -1)
    (grad_hi,) = call(
        after_kernel,
        [
            ord_hi, qkv_weight, gain1, vn, qt, kt, e_hh, gt_hi, inner_hi, amp_hi, part, mix_hi,
        ],
        [(HALF, C)],
        [vm((3 * C, HALF), bf16), vm((HALF, HALF), bf16), vm((HALF, HALF), bf16)],
        "after",
        24,
    )
    to_prev, to_next = call(
        back_kernel, [grad_hi, chip(grad_second), slot], [(CAP, C)] * 2, [], "back"
    )
    back_left = shift(to_prev, -1)
    back_right = shift(to_next, 1)
    (own,) = call(own_kernel, [grad_hi, chip(grad_second), slot], [(N, C)], [], "own")
    (grad_points,) = call(
        final_kernel, [own, chip(back_right), chip(back_left), sender], [(N, C)], [], "final"
    )
    block_out = jnp.concatenate([out_hi, out_second], axis=0)
    return (block_out[None], grad_points[None])


def solution(mesh):
    rows = P(None, ("gx", "gy"), None)
    in_specs = (rows, rows, P(None, ("gx", "gy")), P(), P(), P(), P(), P(), P(), rows)
    return jax.shard_map(
        shards, mesh=mesh, in_specs=in_specs, out_specs=(rows, rows), check_vma=False
    )
```

```python
import functools
import math

import jax
import jax.numpy as jnp
from jax import lax
from jax.experimental import pallas as pl
from jax.experimental.pallas import tpu as pltpu
from jax.sharding import PartitionSpec as P


H = 16
D = 16
C = 256
N = 1024
HALF = 512
CAP = 384
FF = 1024
ROWS = 256
EPS = 1e-05
LOG2E = 1.4426950408889634
SCORE = LOG2E / 4.0
VSCALE = 2.0**-8
UNROLL_BEFORE = 1
UNROLL_FORWARD = 1
UNROLL_BACKWARD = 1
UNROLL_AFTER = 1

bf16 = jnp.bfloat16
f32 = jnp.float32


def dg(a, b, ca, cb):
    return lax.dot_general(a, b, (((ca,), (cb,)), ((), ())), preferred_element_type=f32)


def column(row, count):
    return jnp.transpose(jnp.broadcast_to(row, (128, count)))


def picks_from_column(col, start, width):
    lanes = lax.broadcasted_iota(jnp.int32, col.shape, 1)
    parts = [
        jnp.where(col == lanes + (start + 128 * b), 1.0, 0.0).astype(bf16)
        for b in range(width // 128)
    ]
    return jnp.concatenate(parts, axis=1)


def picks_from_row(row, start, height):
    ids = lax.broadcasted_iota(jnp.int32, (height, row.shape[1]), 0) + start
    return jnp.where(ids == row, 1.0, 0.0).astype(bf16)


def start_copies(pairs, sems):
    copies = [pltpu.make_async_copy(src, dst, sems.at[i]) for i, (src, dst) in enumerate(pairs)]
    for copy in copies:
        copy.start()
    return copies


def gather_kernel(
    points, sender, slot, wqkv, gain1, gain2,
    left, right, points_v, sender_v, slot_v, wqkv_v, gain1_v, gain2_v, sems,
):
    copies = start_copies(
        [
            (sender, sender_v), (points, points_v), (slot, slot_v), (wqkv, wqkv_v),
            (gain1, gain1_v), (gain2, gain2_v),
        ],
        sems,
    )
    copies[0].wait()
    picks = picks_from_column(column(sender_v[...], 2 * CAP), 0, N)
    copies[1].wait()
    rows = dg(picks, points_v[...], 1, 0).astype(bf16)
    left[...] = rows[:CAP]
    right[...] = rows[CAP:]
    for copy in copies[2:]:
        copy.wait()


def order_kernel(points, from_prev, from_next, slot, first, second):
    col = column(slot[...], N)
    rows = dg(picks_from_column(col, 0, N), points[...], 1, 0)
    rows += dg(picks_from_column(col, N, CAP), from_prev[...], 1, 0)
    rows += dg(picks_from_column(col, N + CAP, CAP), from_next[...], 1, 0)
    rows = rows.astype(bf16)
    first[...] = rows[:HALF]
    second[...] = rows[HALF:]


def back_kernel(first, second, slot, to_prev, to_next):
    row = slot[...]
    picks = picks_from_row(row, N, 2 * CAP)
    rows = dg(picks[:, :HALF], first[...], 1, 0) + dg(picks[:, HALF:], second[...], 1, 0)
    rows = rows.astype(bf16)
    to_prev[...] = rows[:CAP]
    to_next[...] = rows[CAP:]


def own_kernel(first, second, slot, out):
    picks = picks_from_row(slot[...], 0, N)
    rows = dg(picks[:, :HALF], first[...], 1, 0) + dg(picks[:, HALF:], second[...], 1, 0)
    out[...] = rows.astype(bf16)


def final_kernel(own, left, right, sender, out):
    picks = picks_from_row(sender[...], 0, N)
    rows = dg(picks[:, :CAP], left[...], 1, 0) + dg(picks[:, CAP:], right[...], 1, 0)
    out[...] = (own[...].astype(f32) + rows).astype(bf16)


def normalize(rows):
    mean = jnp.mean(rows, axis=-1, keepdims=True)
    centered = rows - mean
    spread = jnp.mean(centered * centered, axis=-1, keepdims=True)
    scale = lax.rsqrt(spread + EPS)
    return centered * scale, scale


def normalize_back(grad, unit, scale):
    return scale * (
        grad
        - jnp.mean(grad, axis=-1, keepdims=True)
        - unit * jnp.mean(grad * unit, axis=-1, keepdims=True)
    )


def front(rows, gain, weight):
    unit, _ = normalize(rows.astype(f32))
    return dg((unit * gain).astype(bf16), weight, 1, 0).astype(bf16)


def split_qkv(rows_ref, gain, weight, kn, vn, qt, kt, vt):
    vt[...] = jnp.full(vt.shape, VSCALE, bf16)
    for b in range(HALF // ROWS):
        sl = slice(b * ROWS, (b + 1) * ROWS)
        qkv = front(rows_ref[sl], gain[...], weight[...])
        kn[0, sl] = qkv[:, 256:384]
        kn[1, sl] = qkv[:, 384:512]
        vn[0, sl] = qkv[:, 512:640]
        vn[1, sl] = qkv[:, 640:768]
        flipped = jnp.transpose(qkv)
        qt[:, sl] = flipped[:256]
        kt[:, sl] = flipped[256:512]
        vt[:, :D, sl] = flipped[512:].reshape(H, D, ROWS) * bf16(VSCALE)


def front_back(dt, rows_ref, mix_grad, gain, weight, out):
    for b in range(HALF // ROWS):
        sl = slice(b * ROWS, (b + 1) * ROWS)
        grad_normed = dg(jnp.transpose(dt[:, sl]), weight[...], 1, 1)
        unit, scale = normalize(rows_ref[sl].astype(f32))
        grad = mix_grad[sl] + normalize_back(grad_normed * gain[...], unit, scale)
        out[sl] = grad.astype(bf16)


def head_mask(h):
    return lax.broadcasted_iota(jnp.int32, (HALF, 128), 1) // D == h % 8


def weigh(keys, queries):
    return jnp.exp2(dg(keys, queries, 1, 0) * SCORE).astype(bf16)


def before_kernel(
    ord_hi, wqkv, gain1, cot, kn, vn, qt, kt, vt, e_hh, sums_hh, cot_second, sems
):
    copies = start_copies([(cot.at[pl.ds(HALF, HALF)], cot_second)], sems)
    split_qkv(ord_hi, gain1, wqkv, kn, vn, qt, kt, vt)

    def one_head(h, carry):
        block = h // 8
        keys = jnp.where(head_mask(h), kn[block], bf16(0))
        weights = weigh(keys, qt[pl.ds(block * 128, 128)])
        e_hh[h] = weights
        sums_hh[h] = dg(vt[h], weights, 1, 0)
        return carry

    lax.fori_loop(0, H, one_head, 0, unroll=UNROLL_BEFORE)
    copies[0].wait()


def forward_kernel(
    ord_lo, wqkv, gain1, kn_hi, qt_hi, vt_hi, sums_hh, wproj_h, wfc1_h, wfc2_h, cot_h,
    vn, qt, kt, e_l, e_hl, ot, inv_scr, amp_scr, wproj, wfc1, wfc2, cot_hi,
    kn, vt, sems,
):
    copies = start_copies(
        [(wproj_h, wproj), (wfc1_h, wfc1), (wfc2_h, wfc2), (cot_h.at[pl.ds(0, HALF)], cot_hi)],
        sems,
    )
    split_qkv(ord_lo, gain1, wqkv, kn, vn, qt.at[:, :HALF], kt, vt)
    qt[:, HALF:] = qt_hi[...]

    def forward_head(h, carry):
        block = h // 8
        mask = head_mask(h)
        lanes = pl.ds(block * 128, 128)
        weights = weigh(jnp.where(mask, kn[block], bf16(0)), qt[lanes])
        e_l[h] = weights
        side = weigh(jnp.where(mask, kn_hi[block], bf16(0)), qt[lanes, :HALF])
        e_hl[h] = side
        sums = dg(vt[h], weights, 1, 0)
        sums += jnp.concatenate([dg(vt_hi[h], side, 1, 0), sums_hh[h]], axis=1)
        total = sums[D : D + 1]
        amp = jnp.where(total >= 2.0**40, 2.0**-80, jnp.where(total < 2.0**-40, 2.0**80, 1.0))
        inverse = 1.0 / (total * amp)
        ot[pl.ds(h * D, D)] = (sums[:D] * amp) * inverse
        inv_scr[pl.ds(h * D, D)] = jnp.broadcast_to(inverse * VSCALE, (D, N))
        amp_scr[h] = jnp.broadcast_to(amp, (D, N)).astype(bf16)
        return carry

    lax.fori_loop(0, H, forward_head, 0, unroll=UNROLL_FORWARD)
    for copy in copies:
        copy.wait()


def middle_kernel(
    ord_lo, ord_hi, cot_lo, cot_hi, wproj, wfc1, wfc2, gain2, ot, inv_scr,
    out_lo, out_hi, gt, mix_lo, mix_hi,
):
    for b in range(N // ROWS):
        sl = slice(b * ROWS, (b + 1) * ROWS)
        half = b // 2
        hs = slice((b % 2) * ROWS, (b % 2 + 1) * ROWS)
        attention = jnp.transpose(ot[:, sl].astype(bf16))
        mixed = (ord_lo, ord_hi)[half][hs].astype(f32) + dg(attention, wproj[...], 1, 0)
        unit, scale = normalize(mixed)
        normed = (unit * gain2[...]).astype(bf16)
        pre = dg(normed, wfc1[...], 1, 0)
        cdf = 0.5 * (1.0 + lax.erf(pre * (2.0**-0.5)))
        act = (pre * cdf).astype(bf16)
        (out_lo, out_hi)[half][hs] = (mixed + dg(act, wfc2[...], 1, 0)).astype(bf16)
        cot = (cot_lo, cot_hi)[half][hs]
        grad_act = dg(cot, wfc2[...], 1, 1)
        density = jnp.exp(-0.5 * pre * pre) * (1.0 / math.sqrt(2.0 * math.pi))
        grad_pre = (grad_act * (cdf + pre * density)).astype(bf16)
        grad_normed = dg(grad_pre, wfc1[...], 1, 1)
        grad_mixed = cot.astype(f32) + normalize_back(grad_normed * gain2[...], unit, scale)
        (mix_lo, mix_hi)[half][hs] = grad_mixed
        grad_att = dg(grad_mixed.astype(bf16), wproj[...], 1, 1).astype(bf16)
        gt[:, sl] = (jnp.transpose(grad_att).astype(f32) * inv_scr[:, sl]).astype(bf16)


def backward_kernel(
    ord_lo, wqkv, gain1, vn, vn_hi, qt, kt, kt_hi, e_l, e_hl, ot, amp_scr, gt, mix_lo,
    grad_lo, inner_hi, part,
    dt, p_t, s_t, ph_t, sh_t,
):
    def backward_head(h, carry):
        block = h // 8
        rows = pl.ds(h * D, D)
        rows_k = pl.ds(256 + h * D, D)
        rows_v = pl.ds(512 + h * D, D)
        lanes = pl.ds(block * 128, 128)
        mask = head_mask(h)
        grads = gt[rows]
        inner = jnp.sum(grads.astype(f32) * ot[rows], axis=0, keepdims=True)
        inner_hi[h] = jnp.broadcast_to(inner[:, HALF:], (8, HALF))
        amp = amp_scr[h, :1]
        probs = e_l[h] * amp
        p_t[...] = jnp.transpose(probs)
        side = e_hl[h] * amp[:, :HALF]
        ph_t[...] = jnp.transpose(side)
        values = jnp.where(mask, vn[block], bf16(0))
        scores = probs * (dg(values, gt[lanes], 1, 0) - inner).astype(bf16)
        grad_q = dg(kt[rows], scores, 1, 0)
        values = jnp.where(mask, vn_hi[block], bf16(0))
        side_scores = side * (dg(values, gt[lanes, :HALF], 1, 0) - inner[:, :HALF]).astype(bf16)
        s_t[...] = jnp.transpose(scores)
        sh_t[...] = jnp.transpose(side_scores)
        dt[rows] = ((grad_q[:, :HALF] + dg(kt_hi[rows], side_scores, 1, 0)) * 0.25).astype(bf16)
        part[rows] = grad_q[:, HALF:]
        dt[rows_v] = dg(grads, p_t[...], 1, 0).astype(bf16)
        part[rows_v] = dg(gt[rows, :HALF], ph_t[...], 1, 0)
        dt[rows_k] = (dg(qt[rows], s_t[...], 1, 0) * 0.25).astype(bf16)
        part[rows_k] = dg(qt[rows, :HALF], sh_t[...], 1, 0)
        return carry

    lax.fori_loop(0, H, backward_head, 0, unroll=UNROLL_BACKWARD)
    front_back(dt, ord_lo, mix_lo, gain1, wqkv, grad_lo)


def after_kernel(
    ord_hi, wqkv, gain1, vn, qt, kt, e_hh, gt, inner_hi, amp_hi, part, mix_hi,
    grad_hi, dt, p_t, s_t,
):
    def backward_head(h, carry):
        block = h // 8
        rows = pl.ds(h * D, D)
        rows_k = pl.ds(256 + h * D, D)
        rows_v = pl.ds(512 + h * D, D)
        probs = e_hh[h] * amp_hi[h, :1, HALF:]
        p_t[...] = jnp.transpose(probs)
        values = jnp.where(head_mask(h), vn[block], bf16(0))
        inner = inner_hi[h][:1]
        scores = probs * (dg(values, gt[pl.ds(block * 128, 128), HALF:], 1, 0) - inner).astype(bf16)
        s_t[...] = jnp.transpose(scores)
        dt[rows] = ((part[rows] + dg(kt[rows], scores, 1, 0)) * 0.25).astype(bf16)
        dt[rows_v] = (part[rows_v] + dg(gt[rows, HALF:], p_t[...], 1, 0)).astype(bf16)
        dt[rows_k] = ((part[rows_k] + dg(qt[rows], s_t[...], 1, 0)) * 0.25).astype(bf16)
        return carry

    lax.fori_loop(0, H, backward_head, 0, unroll=UNROLL_AFTER)
    front_back(dt, ord_hi, mix_hi, gain1, wqkv, grad_hi)


vm = pltpu.VMEM


def chip(rows):
    return pltpu.with_memory_space_constraint(rows, pltpu.VMEM)


def call(kernel, operands, far, outs, scratch, limit, sems=0):
    near = pl.BlockSpec(memory_space=pltpu.VMEM)
    away = pl.BlockSpec(memory_space=pltpu.HBM)
    return pl.pallas_call(
        kernel,
        in_specs=[near] * len(operands) + [away] * len(far),
        out_specs=tuple([near] * len(outs)),
        out_shape=tuple(
            o if not isinstance(o, tuple) else jax.ShapeDtypeStruct(o, bf16) for o in outs
        ),
        scratch_shapes=list(scratch) + ([pltpu.SemaphoreType.DMA((sems,))] if sems else []),
        compiler_params=pltpu.CompilerParams(vmem_limit_bytes=limit << 20),
    )(*operands, *[pltpu.with_memory_space_constraint(f, pltpu.HBM) for f in far])


def shift(rows, step):
    axes = ("gx", "gy")
    count = lax.axis_size(axes)
    return lax.ppermute(rows, axes, [(i, (i + step) % count) for i in range(count)])


def shards(
    points, send_rows, recv_slot, norm1_gain, qkv_weight, proj_weight, norm2_gain,
    fc1_weight, fc2_weight, cotangent,
):
    local = points[0]
    sender = send_rows[0]
    slot = recv_slot
    cot = cotangent[0]
    gain1 = norm1_gain.reshape(1, C)
    gain2 = norm2_gain.reshape(1, C)

    half = vm((HALF, C), bf16)
    half_f = vm((HALF, C), f32)
    gain_v = vm((1, C), f32)
    left, right, points_v, sender_v, slot_v, wqkv, gain1, gain2 = call(
        gather_kernel,
        [],
        [local, sender, slot, qkv_weight, gain1, gain2],
        [
            (CAP, C), (CAP, C), vm((N, C), bf16), vm((1, 2 * CAP), jnp.int32),
            vm((1, N), jnp.int32), vm((C, 3 * C), bf16), gain_v, gain_v,
        ],
        [],
        6,
        6,
    )
    from_prev = shift(right, 1)
    from_next = shift(left, -1)
    ord_hi, second = call(
        order_kernel,
        [points_v, chip(from_prev), chip(from_next), slot_v],
        [],
        [half, (HALF, C)],
        [],
        8,
    )
    ord_lo = shift(second, 1)
    natural = vm((2, HALF, 128), bf16)
    flipped = vm((C, HALF), bf16)
    wide = vm((C, N), bf16)
    wide_f = vm((C, N), f32)
    valued = vm((H, 2 * D, HALF), bf16)
    square = vm((H, HALF, HALF), bf16)
    tall = vm((N, HALF), bf16)
    tile = vm((HALF, HALF), bf16)
    kn_hi, vn_hi, qt_hi, kt_hi, vt_hi, e_hh, sums_hh, cot_second = call(
        before_kernel,
        [ord_hi, wqkv, gain1],
        [cot],
        [
            natural, natural, flipped, flipped, valued, square, vm((H, 2 * D, HALF), f32),
            (HALF, C),
        ],
        [],
        6,
        1,
    )
    cot_lo = shift(cot_second, 1)
    vn, qt, kt, e_l, e_hl, ot, inv, amp, wproj, wfc1, wfc2, cot_hi = call(
        forward_kernel,
        [chip(ord_lo), wqkv, gain1, kn_hi, qt_hi, vt_hi, sums_hh],
        [proj_weight, fc1_weight, fc2_weight, cot],
        [
            natural, wide, flipped, vm((H, HALF, N), bf16), square, wide_f, wide_f,
            vm((H, D, N), bf16), vm((C, C), bf16), vm((C, FF), bf16), vm((FF, C), bf16), half,
        ],
        [natural, valued],
        9,
        4,
    )
    out_lo, out_hi, gt, mix_lo, mix_hi = call(
        middle_kernel,
        [chip(ord_lo), ord_hi, chip(cot_lo), cot_hi, wproj, wfc1, wfc2, gain2, ot, inv],
        [],
        [(HALF, C), (HALF, C), wide, half_f, half_f],
        [],
        12,
    )
    out_second = shift(out_lo, -1)
    back = functools.partial(
        call,
        backward_kernel,
        [
            chip(ord_lo), wqkv, gain1, vn, vn_hi, qt, kt, kt_hi, chip(e_l), chip(e_hl), ot, amp, gt, mix_lo,
        ],
        [],
        [(HALF, C), vm((H, 8, HALF), f32), vm((3 * C, HALF), f32)],
        [vm((3 * C, HALF), bf16), tall, tall, tile, tile],
        9,
    )
    grad_lo, inner_hi, part = back()
    grad_second = shift(grad_lo, -1)
    (grad_hi,) = call(
        after_kernel,
        [ord_hi, wqkv, gain1, vn_hi, qt_hi, kt_hi, chip(e_hh), gt, inner_hi, amp, part, mix_hi],
        [],
        [half],
        [vm((3 * C, HALF), bf16), tile, tile],
        6,
    )
    to_prev, to_next = call(
        back_kernel, [grad_hi, chip(grad_second), slot_v], [], [(CAP, C)] * 2, [], 6
    )
    back_left = shift(to_prev, -1)
    back_right = shift(to_next, 1)
    (own,) = call(own_kernel, [grad_hi, chip(grad_second), slot_v], [], [vm((N, C), bf16)], [], 6)
    (grad_points,) = call(
        final_kernel, [own, chip(back_right), chip(back_left), sender_v], [], [(N, C)], [], 6
    )
    block_out = jnp.concatenate([out_hi, out_second], axis=0)
    return (block_out[None], grad_points[None])


def solution(mesh):
    rows = P(None, ("gx", "gy"), None)
    in_specs = (rows, rows, P(None, ("gx", "gy")), P(), P(), P(), P(), P(), P(), rows)

    return jax.shard_map(
        shards, mesh=mesh, in_specs=in_specs, out_specs=(rows, rows), check_vma=False
    )
```

```python
import functools
import math

import jax
import jax.numpy as jnp
from jax import lax
from jax.experimental import pallas as pl
from jax.experimental.pallas import tpu as pltpu
from jax.sharding import PartitionSpec as P


H = 16
D = 16
C = 256
N = 1024
HALF = 512
CAP = 384
FF = 1024
ROWS = 256
EPS = 1e-05
LOG2E = 1.4426950408889634
SCORE = LOG2E / 4.0
VSCALE = 2.0**-8
UNROLL_BEFORE = 4
UNROLL_FORWARD = 2
UNROLL_BACKWARD = 2
UNROLL_AFTER = 4

bf16 = jnp.bfloat16
f32 = jnp.float32


def dg(a, b, ca, cb):
    return lax.dot_general(a, b, (((ca,), (cb,)), ((), ())), preferred_element_type=f32)


def column(row, count):
    return jnp.transpose(jnp.broadcast_to(row, (128, count)))


def picks_from_column(col, start, width):
    lanes = lax.broadcasted_iota(jnp.int32, col.shape, 1)
    parts = [
        jnp.where(col == lanes + (start + 128 * b), 1.0, 0.0).astype(bf16)
        for b in range(width // 128)
    ]
    return jnp.concatenate(parts, axis=1)


def picks_from_row(row, start, height):
    ids = lax.broadcasted_iota(jnp.int32, (height, row.shape[1]), 0) + start
    return jnp.where(ids == row, 1.0, 0.0).astype(bf16)


def start_copies(pairs, sems):
    copies = [pltpu.make_async_copy(src, dst, sems.at[i]) for i, (src, dst) in enumerate(pairs)]
    for copy in copies:
        copy.start()
    return copies


def gather_kernel(
    points, sender, slot, wqkv, gain1, gain2,
    left, right, points_v, sender_v, slot_v, wqkv_v, gain1_v, gain2_v, sems,
):
    copies = start_copies(
        [
            (sender, sender_v), (points, points_v), (slot, slot_v), (wqkv, wqkv_v),
            (gain1, gain1_v), (gain2, gain2_v),
        ],
        sems,
    )
    copies[0].wait()
    picks = picks_from_column(column(sender_v[...], 2 * CAP), 0, N)
    copies[1].wait()
    rows = dg(picks, points_v[...], 1, 0).astype(bf16)
    left[...] = rows[:CAP]
    right[...] = rows[CAP:]
    for copy in copies[2:]:
        copy.wait()


def order_kernel(points, from_prev, from_next, slot, first, second):
    col = column(slot[...], N)
    rows = dg(picks_from_column(col, 0, N), points[...], 1, 0)
    rows += dg(picks_from_column(col, N, CAP), from_prev[...], 1, 0)
    rows += dg(picks_from_column(col, N + CAP, CAP), from_next[...], 1, 0)
    rows = rows.astype(bf16)
    first[...] = rows[:HALF]
    second[...] = rows[HALF:]


def back_kernel(first, second, slot, to_prev, to_next):
    row = slot[...]
    picks = picks_from_row(row, N, 2 * CAP)
    rows = dg(picks[:, :HALF], first[...], 1, 0) + dg(picks[:, HALF:], second[...], 1, 0)
    rows = rows.astype(bf16)
    to_prev[...] = rows[:CAP]
    to_next[...] = rows[CAP:]


def own_kernel(first, second, slot, out):
    picks = picks_from_row(slot[...], 0, N)
    rows = dg(picks[:, :HALF], first[...], 1, 0) + dg(picks[:, HALF:], second[...], 1, 0)
    out[...] = rows.astype(bf16)


def final_kernel(own, left, right, sender, out):
    picks = picks_from_row(sender[...], 0, N)
    rows = dg(picks[:, :CAP], left[...], 1, 0) + dg(picks[:, CAP:], right[...], 1, 0)
    out[...] = (own[...].astype(f32) + rows).astype(bf16)


def normalize(rows):
    mean = jnp.mean(rows, axis=-1, keepdims=True)
    centered = rows - mean
    spread = jnp.mean(centered * centered, axis=-1, keepdims=True)
    scale = lax.rsqrt(spread + EPS)
    return centered * scale, scale


def normalize_back(grad, unit, scale):
    return scale * (
        grad
        - jnp.mean(grad, axis=-1, keepdims=True)
        - unit * jnp.mean(grad * unit, axis=-1, keepdims=True)
    )


def front(rows, gain, weight):
    unit, _ = normalize(rows.astype(f32))
    return dg((unit * gain).astype(bf16), weight, 1, 0).astype(bf16)


def split_qkv(rows_ref, gain, weight, kn, vn, qt, kt, vt):
    vt[...] = jnp.full(vt.shape, VSCALE, bf16)
    for b in range(HALF // ROWS):
        sl = slice(b * ROWS, (b + 1) * ROWS)
        qkv = front(rows_ref[sl], gain[...], weight[...])
        kn[0, sl] = qkv[:, 256:384]
        kn[1, sl] = qkv[:, 384:512]
        vn[0, sl] = qkv[:, 512:640]
        vn[1, sl] = qkv[:, 640:768]
        flipped = jnp.transpose(qkv)
        qt[:, sl] = flipped[:256]
        kt[:, sl] = flipped[256:512]
        vt[:, :D, sl] = flipped[512:].reshape(H, D, ROWS) * bf16(VSCALE)


def front_back(dt, rows_ref, mix_grad, gain, weight, out):
    for b in range(HALF // ROWS):
        sl = slice(b * ROWS, (b + 1) * ROWS)
        grad_normed = dg(jnp.transpose(dt[:, sl]), weight[...], 1, 1)
        unit, scale = normalize(rows_ref[sl].astype(f32))
        grad = mix_grad[sl] + normalize_back(grad_normed * gain[...], unit, scale)
        out[sl] = grad.astype(bf16)


def head_lanes(h):
    lanes = lax.broadcasted_iota(jnp.int32, (1, 128), 1)
    return jnp.where(lanes // D == h % 8, 1.0, 0.0).astype(bf16)


def each_head(unroll, body):
    def step(i, carry):
        for j in range(unroll):
            body(i * unroll + j, j)
        return carry

    lax.fori_loop(0, H // unroll, step, 0)


def weigh(keys, queries):
    return jnp.exp2(dg(keys, queries, 1, 0) * SCORE).astype(bf16)


def before_kernel(
    ord_hi, wqkv, gain1, cot, kn, vn, qt, kt, vt, e_hh, sums_hh, cot_second, sems
):
    copies = start_copies([(cot.at[pl.ds(HALF, HALF)], cot_second)], sems)
    split_qkv(ord_hi, gain1, wqkv, kn, vn, qt, kt, vt)

    def one_head(h, j):
        block = h // 8
        keys = kn[block] * head_lanes(h)
        weights = weigh(keys, qt[pl.ds(block * 128, 128)])
        e_hh[h] = weights
        sums_hh[h] = dg(vt[h], weights, 1, 0)

    each_head(UNROLL_BEFORE, one_head)
    copies[0].wait()


def forward_kernel(
    ord_lo, wqkv, gain1, kn_hi, qt_hi, vt_hi, sums_hh, wproj_h, wfc1_h, wfc2_h, cot_h,
    vn, qt, kt, e_l, e_hl, ot, inv_scr, amp_scr, wproj, wfc1, wfc2, cot_hi,
    kn, vt, sems,
):
    copies = start_copies(
        [(wproj_h, wproj), (wfc1_h, wfc1), (wfc2_h, wfc2), (cot_h.at[pl.ds(0, HALF)], cot_hi)],
        sems,
    )
    split_qkv(ord_lo, gain1, wqkv, kn, vn, qt.at[:, :HALF], kt, vt)
    qt[:, HALF:] = qt_hi[...]

    def forward_head(h, j):
        block = h // 8
        mask = head_lanes(h)
        lanes = pl.ds(block * 128, 128)
        weights = weigh(kn[block] * mask, qt[lanes])
        e_l[h] = weights
        side = weigh(kn_hi[block] * mask, qt[lanes, :HALF])
        e_hl[h] = side
        sums = dg(vt[h], weights, 1, 0)
        sums += jnp.concatenate([dg(vt_hi[h], side, 1, 0), sums_hh[h]], axis=1)
        total = sums[D : D + 1]
        amp = jnp.where(total >= 2.0**40, 2.0**-80, jnp.where(total < 2.0**-40, 2.0**80, 1.0))
        inverse = 1.0 / (total * amp)
        ot[pl.ds(h * D, D)] = (sums[:D] * amp) * inverse
        inv_scr[pl.ds(h * D, D)] = jnp.broadcast_to(inverse * VSCALE, (D, N))
        amp_scr[h] = jnp.broadcast_to(amp, (D, N)).astype(bf16)

    each_head(UNROLL_FORWARD, forward_head)
    for copy in copies:
        copy.wait()


def middle_kernel(
    ord_lo, ord_hi, cot_lo, cot_hi, wproj, wfc1, wfc2, gain2, ot, inv_scr,
    out_lo, out_hi, gt, mix_lo, mix_hi,
):
    for b in range(N // ROWS):
        sl = slice(b * ROWS, (b + 1) * ROWS)
        half = b // 2
        hs = slice((b % 2) * ROWS, (b % 2 + 1) * ROWS)
        attention = jnp.transpose(ot[:, sl].astype(bf16))
        mixed = (ord_lo, ord_hi)[half][hs].astype(f32) + dg(attention, wproj[...], 1, 0)
        unit, scale = normalize(mixed)
        normed = (unit * gain2[...]).astype(bf16)
        pre = dg(normed, wfc1[...], 1, 0)
        cdf = 0.5 * (1.0 + lax.erf(pre * (2.0**-0.5)))
        act = (pre * cdf).astype(bf16)
        (out_lo, out_hi)[half][hs] = (mixed + dg(act, wfc2[...], 1, 0)).astype(bf16)
        cot = (cot_lo, cot_hi)[half][hs]
        grad_act = dg(cot, wfc2[...], 1, 1)
        density = jnp.exp(-0.5 * pre * pre) * (1.0 / math.sqrt(2.0 * math.pi))
        grad_pre = (grad_act * (cdf + pre * density)).astype(bf16)
        grad_normed = dg(grad_pre, wfc1[...], 1, 1)
        grad_mixed = cot.astype(f32) + normalize_back(grad_normed * gain2[...], unit, scale)
        (mix_lo, mix_hi)[half][hs] = grad_mixed
        grad_att = dg(grad_mixed.astype(bf16), wproj[...], 1, 1).astype(bf16)
        gt[:, sl] = (jnp.transpose(grad_att).astype(f32) * inv_scr[:, sl]).astype(bf16)


def backward_kernel(
    ord_lo, wqkv, gain1, vn, vn_hi, qt, kt, kt_hi, e_l, e_hl, ot, amp_scr, gt, mix_lo,
    grad_lo, inner_hi, part,
    dt, p_t, s_t, ph_t, sh_t,
):
    def backward_head(h, j):
        block = h // 8
        rows = pl.ds(h * D, D)
        rows_k = pl.ds(256 + h * D, D)
        rows_v = pl.ds(512 + h * D, D)
        lanes = pl.ds(block * 128, 128)
        mask = head_lanes(h)
        grads = gt[rows]
        inner = jnp.sum(grads.astype(f32) * ot[rows], axis=0, keepdims=True)
        inner_hi[h] = jnp.broadcast_to(inner[:, HALF:], (8, HALF))
        amp = amp_scr[h, :1]
        probs = e_l[h] * amp
        p_t[j] = jnp.transpose(probs)
        side = e_hl[h] * amp[:, :HALF]
        ph_t[j] = jnp.transpose(side)
        values = vn[block] * mask
        scores = probs * (dg(values, gt[lanes], 1, 0) - inner).astype(bf16)
        grad_q = dg(kt[rows], scores, 1, 0)
        values = vn_hi[block] * mask
        side_scores = side * (dg(values, gt[lanes, :HALF], 1, 0) - inner[:, :HALF]).astype(bf16)
        s_t[j] = jnp.transpose(scores)
        sh_t[j] = jnp.transpose(side_scores)
        dt[rows] = ((grad_q[:, :HALF] + dg(kt_hi[rows], side_scores, 1, 0)) * 0.25).astype(bf16)
        part[rows] = grad_q[:, HALF:]
        dt[rows_v] = dg(grads, p_t[j], 1, 0).astype(bf16)
        part[rows_v] = dg(gt[rows, :HALF], ph_t[j], 1, 0)
        dt[rows_k] = (dg(qt[rows], s_t[j], 1, 0) * 0.25).astype(bf16)
        part[rows_k] = dg(qt[rows, :HALF], sh_t[j], 1, 0)

    each_head(UNROLL_BACKWARD, backward_head)
    front_back(dt, ord_lo, mix_lo, gain1, wqkv, grad_lo)


def after_kernel(
    ord_hi, wqkv, gain1, vn, qt, kt, e_hh, gt, inner_hi, amp_hi, part, mix_hi,
    grad_hi, dt, p_t, s_t,
):
    def backward_head(h, j):
        block = h // 8
        rows = pl.ds(h * D, D)
        rows_k = pl.ds(256 + h * D, D)
        rows_v = pl.ds(512 + h * D, D)
        probs = e_hh[h] * amp_hi[h, :1, HALF:]
        p_t[j] = jnp.transpose(probs)
        values = vn[block] * head_lanes(h)
        inner = inner_hi[h][:1]
        scores = probs * (dg(values, gt[pl.ds(block * 128, 128), HALF:], 1, 0) - inner).astype(bf16)
        s_t[j] = jnp.transpose(scores)
        dt[rows] = ((part[rows] + dg(kt[rows], scores, 1, 0)) * 0.25).astype(bf16)
        dt[rows_v] = (part[rows_v] + dg(gt[rows, HALF:], p_t[j], 1, 0)).astype(bf16)
        dt[rows_k] = ((part[rows_k] + dg(qt[rows], s_t[j], 1, 0)) * 0.25).astype(bf16)

    each_head(UNROLL_AFTER, backward_head)
    front_back(dt, ord_hi, mix_hi, gain1, wqkv, grad_hi)


vm = pltpu.VMEM


def chip(rows):
    return pltpu.with_memory_space_constraint(rows, pltpu.VMEM)


def call(kernel, operands, far, outs, scratch, limit, sems=0):
    near = pl.BlockSpec(memory_space=pltpu.VMEM)
    away = pl.BlockSpec(memory_space=pltpu.HBM)
    return pl.pallas_call(
        kernel,
        in_specs=[near] * len(operands) + [away] * len(far),
        out_specs=tuple([near] * len(outs)),
        out_shape=tuple(
            o if not isinstance(o, tuple) else jax.ShapeDtypeStruct(o, bf16) for o in outs
        ),
        scratch_shapes=list(scratch) + ([pltpu.SemaphoreType.DMA((sems,))] if sems else []),
        compiler_params=pltpu.CompilerParams(vmem_limit_bytes=limit << 20),
    )(*operands, *[pltpu.with_memory_space_constraint(f, pltpu.HBM) for f in far])


def shift(rows, step):
    axes = ("gx", "gy")
    count = lax.axis_size(axes)
    return lax.ppermute(rows, axes, [(i, (i + step) % count) for i in range(count)])


def shards(
    points, send_rows, recv_slot, norm1_gain, qkv_weight, proj_weight, norm2_gain,
    fc1_weight, fc2_weight, cotangent,
):
    local = points[0]
    sender = send_rows[0]
    slot = recv_slot
    cot = cotangent[0]
    gain1 = norm1_gain.reshape(1, C)
    gain2 = norm2_gain.reshape(1, C)

    half = vm((HALF, C), bf16)
    half_f = vm((HALF, C), f32)
    gain_v = vm((1, C), f32)
    left, right, points_v, sender_v, slot_v, wqkv, gain1, gain2 = call(
        gather_kernel,
        [],
        [local, sender, slot, qkv_weight, gain1, gain2],
        [
            (CAP, C), (CAP, C), vm((N, C), bf16), vm((1, 2 * CAP), jnp.int32),
            vm((1, N), jnp.int32), vm((C, 3 * C), bf16), gain_v, gain_v,
        ],
        [],
        6,
        6,
    )
    from_prev = shift(right, 1)
    from_next = shift(left, -1)
    ord_hi, second = call(
        order_kernel,
        [points_v, chip(from_prev), chip(from_next), slot_v],
        [],
        [half, (HALF, C)],
        [],
        8,
    )
    ord_lo = shift(second, 1)
    natural = vm((2, HALF, 128), bf16)
    flipped = vm((C, HALF), bf16)
    wide = vm((C, N), bf16)
    wide_f = vm((C, N), f32)
    valued = vm((H, 2 * D, HALF), bf16)
    square = vm((H, HALF, HALF), bf16)
    tall_s = (N, HALF)
    tile_s = (HALF, HALF)
    kn_hi, vn_hi, qt_hi, kt_hi, vt_hi, e_hh, sums_hh, cot_second = call(
        before_kernel,
        [ord_hi, wqkv, gain1],
        [cot],
        [
            natural, natural, flipped, flipped, valued, square, vm((H, 2 * D, HALF), f32),
            (HALF, C),
        ],
        [],
        8,
        1,
    )
    cot_lo = shift(cot_second, 1)
    vn, qt, kt, e_l, e_hl, ot, inv, amp, wproj, wfc1, wfc2, cot_hi = call(
        forward_kernel,
        [chip(ord_lo), wqkv, gain1, kn_hi, qt_hi, vt_hi, sums_hh],
        [proj_weight, fc1_weight, fc2_weight, cot],
        [
            natural, wide, flipped, vm((H, HALF, N), bf16), square, wide_f, wide_f,
            vm((H, D, N), bf16), vm((C, C), bf16), vm((C, FF), bf16), vm((FF, C), bf16), half,
        ],
        [natural, valued],
        13,
        4,
    )
    out_lo, out_hi, gt, mix_lo, mix_hi = call(
        middle_kernel,
        [chip(ord_lo), ord_hi, chip(cot_lo), cot_hi, wproj, wfc1, wfc2, gain2, ot, inv],
        [],
        [(HALF, C), (HALF, C), wide, half_f, half_f],
        [],
        12,
    )
    out_second = shift(out_lo, -1)
    back = functools.partial(
        call,
        backward_kernel,
        [
            chip(ord_lo), wqkv, gain1, vn, vn_hi, qt, kt, kt_hi, chip(e_l), chip(e_hl), ot, amp, gt, mix_lo,
        ],
        [],
        [(HALF, C), vm((H, 8, HALF), f32), vm((3 * C, HALF), f32)],
        [vm((3 * C, HALF), bf16)] + [vm((UNROLL_BACKWARD,) + t, bf16) for t in (tall_s, tall_s, tile_s, tile_s)],
        14,
    )
    grad_lo, inner_hi, part = back()
    grad_second = shift(grad_lo, -1)
    (grad_hi,) = call(
        after_kernel,
        [ord_hi, wqkv, gain1, vn_hi, qt_hi, kt_hi, chip(e_hh), gt, inner_hi, amp, part, mix_hi],
        [],
        [half],
        [vm((3 * C, HALF), bf16)] + [vm((UNROLL_AFTER,) + tile_s, bf16)] * 2,
        11,
    )
    to_prev, to_next = call(
        back_kernel, [grad_hi, chip(grad_second), slot_v], [], [(CAP, C)] * 2, [], 6
    )
    back_left = shift(to_prev, -1)
    back_right = shift(to_next, 1)
    (own,) = call(own_kernel, [grad_hi, chip(grad_second), slot_v], [], [vm((N, C), bf16)], [], 6)
    (grad_points,) = call(
        final_kernel, [own, chip(back_right), chip(back_left), sender_v], [], [(N, C)], [], 6
    )
    block_out = jnp.concatenate([out_hi, out_second], axis=0)
    return (block_out[None], grad_points[None])


def solution(mesh):
    rows = P(None, ("gx", "gy"), None)
    in_specs = (rows, rows, P(None, ("gx", "gy")), P(), P(), P(), P(), P(), P(), rows)

    return jax.shard_map(
        shards, mesh=mesh, in_specs=in_specs, out_specs=(rows, rows), check_vma=False
    )
```

```python
import functools
import math

import jax
import jax.numpy as jnp
from jax import lax
from jax.experimental import pallas as pl
from jax.experimental.pallas import tpu as pltpu
from jax.sharding import PartitionSpec as P


H = 16
D = 16
C = 256
N = 1024
HALF = 512
CAP = 384
FF = 1024
ROWS = 256
EPS = 1e-05
LOG2E = 1.4426950408889634
SCORE = LOG2E / 4.0
VSCALE = 2.0**-8
UNROLL_BEFORE = 4
UNROLL_FORWARD = 4
UNROLL_BACKWARD = 2
UNROLL_AFTER = 4

bf16 = jnp.bfloat16
f32 = jnp.float32


def dg(a, b, ca, cb):
    return lax.dot_general(a, b, (((ca,), (cb,)), ((), ())), preferred_element_type=f32)


def column(row, count):
    return jnp.transpose(jnp.broadcast_to(row, (128, count)))


def picks_from_column(col, start, width):
    lanes = lax.broadcasted_iota(jnp.int32, col.shape, 1)
    parts = [
        jnp.where(col == lanes + (start + 128 * b), 1.0, 0.0).astype(bf16)
        for b in range(width // 128)
    ]
    return jnp.concatenate(parts, axis=1)


def picks_from_row(row, start, height):
    ids = lax.broadcasted_iota(jnp.int32, (height, row.shape[1]), 0) + start
    return jnp.where(ids == row, 1.0, 0.0).astype(bf16)


def start_copies(pairs, sems):
    copies = [pltpu.make_async_copy(src, dst, sems.at[i]) for i, (src, dst) in enumerate(pairs)]
    for copy in copies:
        copy.start()
    return copies


def gather_kernel(
    points, sender, slot, wqkv, gain1, gain2,
    left, right, points_v, sender_v, slot_v, wqkv_v, gain1_v, gain2_v, sems,
):
    copies = start_copies(
        [
            (sender, sender_v), (points, points_v), (slot, slot_v), (wqkv, wqkv_v),
            (gain1, gain1_v), (gain2, gain2_v),
        ],
        sems,
    )
    copies[0].wait()
    picks = picks_from_column(column(sender_v[...], 2 * CAP), 0, N)
    copies[1].wait()
    rows = dg(picks, points_v[...], 1, 0).astype(bf16)
    left[...] = rows[:CAP]
    right[...] = rows[CAP:]
    for copy in copies[2:]:
        copy.wait()


def plan_kernel(points, slot, rows, picks):
    col = column(slot[...], N)
    rows[...] = dg(picks_from_column(col, 0, N), points[...], 1, 0).astype(bf16)
    picks[...] = picks_from_column(col, N, 2 * CAP)


def order_kernel(own, picks, from_prev, from_next, first, second):
    rows = dg(picks[:, :CAP], from_prev[...], 1, 0) + dg(picks[:, CAP:], from_next[...], 1, 0)
    rows = (rows + own[...].astype(f32)).astype(bf16)
    first[...] = rows[:HALF]
    second[...] = rows[HALF:]


def back_kernel(first, second, slot, to_prev, to_next):
    row = slot[...]
    picks = picks_from_row(row, N, 2 * CAP)
    rows = dg(picks[:, :HALF], first[...], 1, 0) + dg(picks[:, HALF:], second[...], 1, 0)
    rows = rows.astype(bf16)
    to_prev[...] = rows[:CAP]
    to_next[...] = rows[CAP:]


def own_kernel(first, second, slot, sender, out, picks_out):
    picks = picks_from_row(slot[...], 0, N)
    rows = dg(picks[:, :HALF], first[...], 1, 0) + dg(picks[:, HALF:], second[...], 1, 0)
    out[...] = rows.astype(bf16)
    picks_out[...] = picks_from_row(sender[...], 0, N)


def final_kernel(own, left, right, picks, out):
    rows = dg(picks[:, :CAP], left[...], 1, 0) + dg(picks[:, CAP:], right[...], 1, 0)
    out[...] = (own[...].astype(f32) + rows).astype(bf16)


def normalize(rows):
    mean = jnp.mean(rows, axis=-1, keepdims=True)
    centered = rows - mean
    spread = jnp.mean(centered * centered, axis=-1, keepdims=True)
    scale = lax.rsqrt(spread + EPS)
    return centered * scale, scale


def normalize_back(grad, unit, scale):
    return scale * (
        grad
        - jnp.mean(grad, axis=-1, keepdims=True)
        - unit * jnp.mean(grad * unit, axis=-1, keepdims=True)
    )


def front(rows, gain, weight):
    unit, _ = normalize(rows.astype(f32))
    return dg((unit * gain).astype(bf16), weight, 1, 0).astype(bf16)


def split_qkv(rows_ref, gain, weight, kn, vn, qt, kt, vt):
    vt[...] = jnp.full(vt.shape, VSCALE, bf16)
    for b in range(HALF // ROWS):
        sl = slice(b * ROWS, (b + 1) * ROWS)
        qkv = front(rows_ref[sl], gain[...], weight[...])
        kn[0, sl] = qkv[:, 256:384]
        kn[1, sl] = qkv[:, 384:512]
        vn[0, sl] = qkv[:, 512:640]
        vn[1, sl] = qkv[:, 640:768]
        flipped = jnp.transpose(qkv)
        qt[:, sl] = flipped[:256]
        kt[:, sl] = flipped[256:512]
        vt[:, :D, sl] = flipped[512:].reshape(H, D, ROWS) * bf16(VSCALE)


def front_back(dt, rows_ref, mix_grad, gain, weight, out):
    for b in range(HALF // ROWS):
        sl = slice(b * ROWS, (b + 1) * ROWS)
        grad_normed = dg(jnp.transpose(dt[:, sl]), weight[...], 1, 1)
        unit, scale = normalize(rows_ref[sl].astype(f32))
        grad = mix_grad[sl] + normalize_back(grad_normed * gain[...], unit, scale)
        out[sl] = grad.astype(bf16)


def head_lanes(h):
    lanes = lax.broadcasted_iota(jnp.int32, (1, 128), 1)
    return jnp.where(lanes // D == h % 8, 1.0, 0.0).astype(bf16)


def each_head(unroll, body):
    def step(i, carry):
        for j in range(unroll):
            body(i * unroll + j, j)
        return carry

    lax.fori_loop(0, H // unroll, step, 0)


def weigh(keys, queries):
    return jnp.exp2(dg(keys, queries, 1, 0) * SCORE).astype(bf16)


def before_kernel(
    ord_hi, wqkv, gain1, cot, kn, vn, qt, kt, vt, e_hh, sums_hh, cot_second, sems
):
    copies = start_copies([(cot.at[pl.ds(HALF, HALF)], cot_second)], sems)
    split_qkv(ord_hi, gain1, wqkv, kn, vn, qt, kt, vt)

    def one_head(h, j):
        block = h // 8
        keys = kn[block] * head_lanes(h)
        weights = weigh(keys, qt[pl.ds(block * 128, 128)])
        e_hh[h] = weights
        sums_hh[h] = dg(vt[h], weights, 1, 0)

    each_head(UNROLL_BEFORE, one_head)
    copies[0].wait()


def forward_kernel(
    ord_lo, wqkv, gain1, kn_hi, qt_hi, vt_hi, sums_hh, wproj_h, wfc1_h, wfc2_h, cot_h,
    vn, qt, kt, e_l, e_hl, ot, inv_scr, amp_scr, wproj, wfc1, wfc2, cot_hi,
    kn, vt, sems,
):
    copies = start_copies(
        [(wproj_h, wproj), (wfc1_h, wfc1), (wfc2_h, wfc2), (cot_h.at[pl.ds(0, HALF)], cot_hi)],
        sems,
    )
    split_qkv(ord_lo, gain1, wqkv, kn, vn, qt.at[:, :HALF], kt, vt)
    qt[:, HALF:] = qt_hi[...]

    def forward_head(h, j):
        block = h // 8
        mask = head_lanes(h)
        lanes = pl.ds(block * 128, 128)
        weights = weigh(kn[block] * mask, qt[lanes])
        e_l[h] = weights
        side = weigh(kn_hi[block] * mask, qt[lanes, :HALF])
        e_hl[h] = side
        sums = dg(vt[h], weights, 1, 0)
        sums += jnp.concatenate([dg(vt_hi[h], side, 1, 0), sums_hh[h]], axis=1)
        total = sums[D : D + 1]
        amp = jnp.where(total >= 2.0**40, 2.0**-80, jnp.where(total < 2.0**-40, 2.0**80, 1.0))
        inverse = 1.0 / (total * amp)
        ot[pl.ds(h * D, D)] = (sums[:D] * amp) * inverse
        inv_scr[pl.ds(h * D, D)] = jnp.broadcast_to(inverse * VSCALE, (D, N))
        amp_scr[h] = jnp.broadcast_to(amp, (D, N)).astype(bf16)

    each_head(UNROLL_FORWARD, forward_head)
    for copy in copies:
        copy.wait()


def middle_kernel(
    ord_lo, ord_hi, cot_lo, cot_hi, wproj, wfc1, wfc2, gain2, ot, inv_scr,
    out_lo, out_hi, gt, mix_lo, mix_hi,
):
    for b in range(N // ROWS):
        sl = slice(b * ROWS, (b + 1) * ROWS)
        half = b // 2
        hs = slice((b % 2) * ROWS, (b % 2 + 1) * ROWS)
        attention = jnp.transpose(ot[:, sl].astype(bf16))
        mixed = (ord_lo, ord_hi)[half][hs].astype(f32) + dg(attention, wproj[...], 1, 0)
        unit, scale = normalize(mixed)
        normed = (unit * gain2[...]).astype(bf16)
        pre = dg(normed, wfc1[...], 1, 0)
        cdf = 0.5 * (1.0 + lax.erf(pre * (2.0**-0.5)))
        act = (pre * cdf).astype(bf16)
        (out_lo, out_hi)[half][hs] = (mixed + dg(act, wfc2[...], 1, 0)).astype(bf16)
        cot = (cot_lo, cot_hi)[half][hs]
        grad_act = dg(cot, wfc2[...], 1, 1)
        density = jnp.exp(-0.5 * pre * pre) * (1.0 / math.sqrt(2.0 * math.pi))
        grad_pre = (grad_act * (cdf + pre * density)).astype(bf16)
        grad_normed = dg(grad_pre, wfc1[...], 1, 1)
        grad_mixed = cot.astype(f32) + normalize_back(grad_normed * gain2[...], unit, scale)
        (mix_lo, mix_hi)[half][hs] = grad_mixed
        grad_att = dg(grad_mixed.astype(bf16), wproj[...], 1, 1).astype(bf16)
        gt[:, sl] = (jnp.transpose(grad_att).astype(f32) * inv_scr[:, sl]).astype(bf16)


def backward_kernel(
    ord_lo, wqkv, gain1, vn, vn_hi, qt, kt, kt_hi, e_l, e_hl, ot, amp_scr, gt, mix_lo,
    grad_lo, inner_hi, part,
    dt, p_t, s_t, ph_t, sh_t,
):
    def backward_head(h, j):
        block = h // 8
        rows = pl.ds(h * D, D)
        rows_k = pl.ds(256 + h * D, D)
        rows_v = pl.ds(512 + h * D, D)
        lanes = pl.ds(block * 128, 128)
        mask = head_lanes(h)
        grads = gt[rows]
        inner = jnp.sum(grads.astype(f32) * ot[rows], axis=0, keepdims=True)
        inner_hi[h] = jnp.broadcast_to(inner[:, HALF:], (8, HALF))
        amp = amp_scr[h, :1]
        probs = e_l[h] * amp
        p_t[j] = jnp.transpose(probs)
        side = e_hl[h] * amp[:, :HALF]
        ph_t[j] = jnp.transpose(side)
        values = vn[block] * mask
        scores = probs * (dg(values, gt[lanes], 1, 0) - inner).astype(bf16)
        grad_q = dg(kt[rows], scores, 1, 0)
        values = vn_hi[block] * mask
        side_scores = side * (dg(values, gt[lanes, :HALF], 1, 0) - inner[:, :HALF]).astype(bf16)
        s_t[j] = jnp.transpose(scores)
        sh_t[j] = jnp.transpose(side_scores)
        dt[rows] = ((grad_q[:, :HALF] + dg(kt_hi[rows], side_scores, 1, 0)) * 0.25).astype(bf16)
        part[rows] = grad_q[:, HALF:]
        dt[rows_v] = dg(grads, p_t[j], 1, 0).astype(bf16)
        part[rows_v] = dg(gt[rows, :HALF], ph_t[j], 1, 0)
        dt[rows_k] = (dg(qt[rows], s_t[j], 1, 0) * 0.25).astype(bf16)
        part[rows_k] = dg(qt[rows, :HALF], sh_t[j], 1, 0)

    each_head(UNROLL_BACKWARD, backward_head)
    front_back(dt, ord_lo, mix_lo, gain1, wqkv, grad_lo)


def after_kernel(
    ord_hi, wqkv, gain1, vn, qt, kt, e_hh, gt, inner_hi, amp_hi, part, mix_hi,
    grad_hi, dt, p_t, s_t,
):
    def backward_head(h, j):
        block = h // 8
        rows = pl.ds(h * D, D)
        rows_k = pl.ds(256 + h * D, D)
        rows_v = pl.ds(512 + h * D, D)
        probs = e_hh[h] * amp_hi[h, :1, HALF:]
        p_t[j] = jnp.transpose(probs)
        values = vn[block] * head_lanes(h)
        inner = inner_hi[h][:1]
        scores = probs * (dg(values, gt[pl.ds(block * 128, 128), HALF:], 1, 0) - inner).astype(bf16)
        s_t[j] = jnp.transpose(scores)
        dt[rows] = ((part[rows] + dg(kt[rows], scores, 1, 0)) * 0.25).astype(bf16)
        dt[rows_v] = (part[rows_v] + dg(gt[rows, HALF:], p_t[j], 1, 0)).astype(bf16)
        dt[rows_k] = ((part[rows_k] + dg(qt[rows], s_t[j], 1, 0)) * 0.25).astype(bf16)

    each_head(UNROLL_AFTER, backward_head)
    front_back(dt, ord_hi, mix_hi, gain1, wqkv, grad_hi)


vm = pltpu.VMEM


def chip(rows):
    return pltpu.with_memory_space_constraint(rows, pltpu.VMEM)


def call(kernel, operands, far, outs, scratch, limit, sems=0):
    near = pl.BlockSpec(memory_space=pltpu.VMEM)
    away = pl.BlockSpec(memory_space=pltpu.HBM)
    return pl.pallas_call(
        kernel,
        in_specs=[near] * len(operands) + [away] * len(far),
        out_specs=tuple([near] * len(outs)),
        out_shape=tuple(
            o if not isinstance(o, tuple) else jax.ShapeDtypeStruct(o, bf16) for o in outs
        ),
        scratch_shapes=list(scratch) + ([pltpu.SemaphoreType.DMA((sems,))] if sems else []),
        compiler_params=pltpu.CompilerParams(vmem_limit_bytes=limit << 20),
    )(*operands, *[pltpu.with_memory_space_constraint(f, pltpu.HBM) for f in far])


def shift(rows, step):
    axes = ("gx", "gy")
    count = lax.axis_size(axes)
    return lax.ppermute(rows, axes, [(i, (i + step) % count) for i in range(count)])


def shards(
    points, send_rows, recv_slot, norm1_gain, qkv_weight, proj_weight, norm2_gain,
    fc1_weight, fc2_weight, cotangent,
):
    local = points[0]
    sender = send_rows[0]
    slot = recv_slot
    cot = cotangent[0]
    gain1 = norm1_gain.reshape(1, C)
    gain2 = norm2_gain.reshape(1, C)

    half = vm((HALF, C), bf16)
    half_f = vm((HALF, C), f32)
    gain_v = vm((1, C), f32)
    left, right, points_v, sender_v, slot_v, wqkv, gain1, gain2 = call(
        gather_kernel,
        [],
        [local, sender, slot, qkv_weight, gain1, gain2],
        [
            (CAP, C), (CAP, C), vm((N, C), bf16), vm((1, 2 * CAP), jnp.int32),
            vm((1, N), jnp.int32), vm((C, 3 * C), bf16), gain_v, gain_v,
        ],
        [],
        6,
        6,
    )
    from_prev = shift(right, 1)
    from_next = shift(left, -1)
    own_rows, arrived = call(
        plan_kernel, [points_v, slot_v], [], [vm((N, C), bf16), vm((N, 2 * CAP), bf16)], [], 8
    )
    ord_hi, second = call(
        order_kernel,
        [own_rows, arrived, chip(from_prev), chip(from_next)],
        [],
        [half, (HALF, C)],
        [],
        8,
    )
    ord_lo = shift(second, 1)
    natural = vm((2, HALF, 128), bf16)
    flipped = vm((C, HALF), bf16)
    wide = vm((C, N), bf16)
    wide_f = vm((C, N), f32)
    valued = vm((H, 2 * D, HALF), bf16)
    square = vm((H, HALF, HALF), bf16)
    tall_s = (N, HALF)
    tile_s = (HALF, HALF)
    kn_hi, vn_hi, qt_hi, kt_hi, vt_hi, e_hh, sums_hh, cot_second = call(
        before_kernel,
        [ord_hi, wqkv, gain1],
        [cot],
        [
            natural, natural, flipped, flipped, valued, square, vm((H, 2 * D, HALF), f32),
            (HALF, C),
        ],
        [],
        8,
        1,
    )
    cot_lo = shift(cot_second, 1)
    vn, qt, kt, e_l, e_hl, ot, inv, amp, wproj, wfc1, wfc2, cot_hi = call(
        forward_kernel,
        [chip(ord_lo), wqkv, gain1, kn_hi, qt_hi, vt_hi, sums_hh],
        [proj_weight, fc1_weight, fc2_weight, cot],
        [
            natural, wide, flipped, vm((H, HALF, N), bf16), square, wide_f, wide_f,
            vm((H, D, N), bf16), vm((C, C), bf16), vm((C, FF), bf16), vm((FF, C), bf16), half,
        ],
        [natural, valued],
        14,
        4,
    )
    out_lo, out_hi, gt, mix_lo, mix_hi = call(
        middle_kernel,
        [chip(ord_lo), ord_hi, chip(cot_lo), cot_hi, wproj, wfc1, wfc2, gain2, ot, inv],
        [],
        [(HALF, C), (HALF, C), wide, half_f, half_f],
        [],
        12,
    )
    out_second = shift(out_lo, -1)
    back = functools.partial(
        call,
        backward_kernel,
        [
            chip(ord_lo), wqkv, gain1, vn, vn_hi, qt, kt, kt_hi, chip(e_l), chip(e_hl), ot, amp, gt, mix_lo,
        ],
        [],
        [(HALF, C), vm((H, 8, HALF), f32), vm((3 * C, HALF), f32)],
        [vm((3 * C, HALF), bf16)] + [vm((UNROLL_BACKWARD,) + t, bf16) for t in (tall_s, tall_s, tile_s, tile_s)],
        14,
    )
    grad_lo, inner_hi, part = back()
    grad_second = shift(grad_lo, -1)
    (grad_hi,) = call(
        after_kernel,
        [ord_hi, wqkv, gain1, vn_hi, qt_hi, kt_hi, chip(e_hh), gt, inner_hi, amp, part, mix_hi],
        [],
        [half],
        [vm((3 * C, HALF), bf16)] + [vm((UNROLL_AFTER,) + tile_s, bf16)] * 2,
        11,
    )
    to_prev, to_next = call(
        back_kernel, [grad_hi, chip(grad_second), slot_v], [], [(CAP, C)] * 2, [], 6
    )
    back_left = shift(to_prev, -1)
    back_right = shift(to_next, 1)
    own, returning = call(
        own_kernel,
        [grad_hi, chip(grad_second), slot_v, sender_v],
        [],
        [vm((N, C), bf16), vm((N, 2 * CAP), bf16)],
        [],
        8,
    )
    (grad_points,) = call(
        final_kernel, [own, chip(back_right), chip(back_left), returning], [], [(N, C)], [], 6
    )
    block_out = jnp.concatenate([out_hi, out_second], axis=0)
    return (block_out[None], grad_points[None])


def solution(mesh):
    rows = P(None, ("gx", "gy"), None)
    in_specs = (rows, rows, P(None, ("gx", "gy")), P(), P(), P(), P(), P(), P(), rows)

    return jax.shard_map(
        shards, mesh=mesh, in_specs=in_specs, out_specs=(rows, rows), check_vma=False
    )
```
